128 devices in a mesh: blk: 64 (over x, z, y_lo, core), rep: 2 (over y_hi).
Axes of the slice: x: 4, y: 4 (y_hi: 2, y_lo: 2; y = y_hi * 2 + y_lo), z: 4, core: 2. Of those that a mesh axis runs over, the one named last changes fastest.
Arguments:
- features: bfloat16 [16384, 128], P('blk'), may hold values from -6 to 6
- tile_values: bfloat16 [64, 64, 16, 128, 128], P('blk', 'rep'), may hold values from -0.046875 to 0.046875
- tile_target: int32 [64, 64, 16], P('blk', 'rep'), may hold values from 0 to 1
- tile_source: int32 [64, 64, 16], P('blk', 'rep'), may hold values from 0 to 1
- tile_count: int32 [64, 64], P('blk', 'rep'), may hold values from 0 to 16, as said below
- hub_list: int32 [64, 64, 16], P('blk'), may hold values from 0 to 255
- hub_count: int32 [64, 64], P('blk'), may hold values from 0 to 16, as said below
- hub_weight: bfloat16 [64, 16, 16384], P(None, None, 'blk'), may hold values from -0.1875 to 0.1875
- self_weight: bfloat16 [128, 256], P(None, 'rep'), may hold values from -0.5 to 0.5
- neighbor_weight: bfloat16 [128, 256], P(None, 'rep'), may hold values from -0.5 to 0.5
- bias: float32 [256], P('rep'), may hold values from -3 to 3
- cotangent: bfloat16 [16384, 256], P('blk', 'rep'), may hold values from -6 to 6
Outputs:
- output: bfloat16 [16384, 256], P('blk', 'rep')
- grad_input: bfloat16 [16384, 128], P('blk')
- grad_self: float32 [128, 256], P(None, 'rep')
- grad_neighbor: float32 [128, 256], P(None, 'rep')
- grad_bias: float32 [256], P('rep')
The draws below stay inside these ranges and needn't reach their ends.
Inputs may be any that keep to these rules, and one draw needn't show every extreme that they name: Slots at or beyond tile_count of a pair of blocks carry values that no output reads. Offset 0 of every destination block has all 16 slots live; some destination blocks may have many slots live at every offset. Coordinates may repeat within a pair; their terms add. `hub_list`: entries may repeat within one list; slots at or beyond hub_count are unused. `hub_count`: every sending block s uses all 16 slots for the reading block (s + 1) mod 64.
All inputs are finite; a program needn't handle non-finite values.
Results may differ from the reference program's by a relative error of at most 0.0056.
Values may be sent and summed in bfloat16 or wider, within the bound.
No kernel may reach another device: no remote copies, remote signals or barrier semaphores. Data moves between devices by JAX's collectives and lax.ppermute only.
A program may use at most 64 MiB of HBM per device.

```python
import math
import jax
import jax.numpy as jnp
from jax import lax

ROWS_DEV = 256
F = 128
HID = 256
TILE = 128
SLOTS = 16
HUB_MOST = 16
BLOCKS = 64
NODES = 16384
TILE_ROWS = 2


def draw_tile_count(key, part):
    heavy_rows = jax.random.randint(jax.random.fold_in(key, 11), (BLOCKS, 1), 0, 8) == 0
    base_counts = jax.random.randint(jax.random.fold_in(key, 12), (BLOCKS, BLOCKS), 0, 5)
    heavy_counts = jax.random.randint(jax.random.fold_in(key, 13), (BLOCKS, BLOCKS), SLOTS // 2, SLOTS + 1)
    counts = jnp.where(heavy_rows, heavy_counts, jnp.minimum(base_counts, SLOTS))
    counts = counts.at[:, 0].set(SLOTS)
    return counts.astype(jnp.int32)


def draw_hub_count(key, part):
    counts = jax.random.randint(jax.random.fold_in(key, 21), (BLOCKS, BLOCKS), 0, HUB_MOST + 1)
    next_reader = (jnp.arange(BLOCKS)[:, None] + 1) % BLOCKS == jnp.arange(BLOCKS)[None, :]
    return jnp.where(next_reader, HUB_MOST, counts).astype(jnp.int32)


def place_ends(drawn, own_key, smallest, largest):
    index_at = [jax.random.randint(jax.random.fold_in(own_key, axis), (), 0, length) for axis, length in enumerate(drawn.shape)]
    main_axis = drawn.shape.index(max(drawn.shape))
    neighbour = index_at[:main_axis] + [(index_at[main_axis] + 1) % drawn.shape[main_axis]] + index_at[main_axis + 1:]
    return drawn.at[tuple(index_at)].set(smallest).at[tuple(neighbour)].set(largest)


def block_levels(stream_key, shape, pieces, low, largest):
    loudness = 1.0
    for position, shards_of in pieces:
        steps = jax.random.uniform(jax.random.fold_in(jax.random.fold_in(stream_key, 6), position), (shards_of,), jnp.float32, low / len(pieces), largest / len(pieces))
        loudness = loudness * jnp.repeat(jnp.exp(steps), shape[position] // shards_of).reshape((-1,) + (1,) * (len(shape) - 1 - position))
    return loudness


def scatter_about(stream_key, extent, scale, reach, split=(), kind=jnp.bfloat16):
    loudness = block_levels(stream_key, extent, split, -0.22, 0.18) if split else 1.0
    entries = jax.random.normal(stream_key, extent, jnp.float32) * scale * loudness
    return jnp.minimum(jnp.maximum(entries, -reach), reach).astype(kind)


def setup_inputs(seed: int = 0) -> dict:
    key_of = jax.random.split(jax.random.key(seed), 13)
    return {
        "features": scatter_about(key_of[0], (NODES, F), 1.0, 6.0, ((0, 64),)),
        "tile_values": scatter_about(key_of[1], (BLOCKS, BLOCKS, SLOTS, TILE, TILE), (BLOCKS * 4 * TILE // TILE_ROWS) ** -0.5, 0.046875, ((0, 64), (1, 2))),
        "tile_target": place_ends(jax.random.randint(key_of[2], (BLOCKS, BLOCKS, SLOTS), 0, TILE_ROWS), jax.random.fold_in(key_of[2], 1), 0, TILE_ROWS - 1).astype(jnp.int32),
        "tile_source": place_ends(jax.random.randint(key_of[3], (BLOCKS, BLOCKS, SLOTS), 0, TILE_ROWS), jax.random.fold_in(key_of[3], 1), 0, TILE_ROWS - 1).astype(jnp.int32),
        "tile_count": draw_tile_count(jax.random.fold_in(key_of[12], 71), 0),
        "hub_list": place_ends(jax.random.randint(key_of[5], (BLOCKS, BLOCKS, HUB_MOST), 0, ROWS_DEV), jax.random.fold_in(key_of[5], 1), 0, ROWS_DEV - 1).astype(jnp.int32),
        "hub_count": draw_hub_count(jax.random.fold_in(key_of[12], 71), 0),
        "hub_weight": scatter_about(key_of[7], (BLOCKS, HUB_MOST, NODES), (BLOCKS * HUB_MOST) ** -0.5, 0.1875, ((2, 64),)),
        "self_weight": scatter_about(key_of[8], (F, HID), F ** -0.5, 0.5, ((1, 2),)),
        "neighbor_weight": scatter_about(key_of[9], (F, HID), F ** -0.5, 0.5, ((1, 2),)),
        "bias": scatter_about(key_of[10], (HID,), 0.5, 3.0, ((0, 2),), jnp.float32),
        "cotangent": scatter_about(key_of[11], (NODES, HID), 1.0, 6.0, ((0, 64), (1, 2))),
    }


def reference(features, tile_values, tile_target, tile_source, tile_count, hub_list, hub_count, hub_weight, self_weight, neighbor_weight, bias, cotangent):
    blocks = tile_count.shape[0]
    node_count, feature_width = features.shape
    rows_dev = node_count // blocks
    tile_size = tile_values.shape[-1]
    tile_rows = rows_dev // tile_size
    slot_ids = jnp.arange(tile_values.shape[2], dtype=jnp.int32)
    hub_ids = jnp.arange(hub_list.shape[2], dtype=jnp.int32)
    sender_base = (jnp.arange(blocks, dtype=jnp.int32) * rows_dev)[:, None]
    feature_tiles = features.reshape(blocks, tile_rows, tile_size, feature_width)
    highest = lax.Precision.HIGHEST

    def block_terms(target, offset):
        source = (target - offset) % blocks
        active = (slot_ids < tile_count[target, offset]).astype(jnp.float32)
        return (source, tile_values[target, offset].astype(jnp.float32), active)

    def hub_terms(target):
        start = (target * rows_dev).astype(jnp.int32)
        weights = lax.dynamic_slice_in_dim(hub_weight, start, rows_dev, 2).astype(jnp.float32)
        hub_active = hub_ids[None, :] < hub_count[:, target][:, None]
        hub_rows = (sender_base + hub_list[:, target, :]).astype(jnp.int32)
        return (weights, hub_active, hub_rows)

    def aggregate_block(target):

        def one_offset(offset, totals):
            source, tile_block, active = block_terms(target, offset)
            picked = feature_tiles[source][tile_source[target, offset]].astype(jnp.float32)
            products = jnp.einsum('jab,jbf->jaf', tile_block, picked, precision=highest)
            placer = jax.nn.one_hot(tile_target[target, offset], tile_rows, dtype=jnp.float32) * active[:, None]
            return totals + jnp.einsum('jt,jaf->taf', placer, products, precision=highest)
        totals = lax.fori_loop(0, blocks, one_offset, jnp.zeros((tile_rows, tile_size, feature_width), jnp.float32))
        weights, hub_active, hub_rows = hub_terms(target)
        picked_rows = features[hub_rows].astype(jnp.float32)
        picked_rows = jnp.where(hub_active[:, :, None], picked_rows, jnp.zeros((), jnp.float32))
        hub_part = jnp.einsum('sjn,sjf->nf', weights, picked_rows, precision=highest)
        return totals.reshape(rows_dev, feature_width) + hub_part
    neighborhood = lax.map(aggregate_block, jnp.arange(blocks, dtype=jnp.int32))
    aggregate = neighborhood.reshape(node_count, feature_width).astype(jnp.bfloat16)
    pre_activation = jnp.dot(features, self_weight, preferred_element_type=jnp.float32) + jnp.dot(aggregate, neighbor_weight, preferred_element_type=jnp.float32) + bias
    output = jax.nn.silu(pre_activation).astype(jnp.bfloat16)
    gate_value = jax.nn.sigmoid(pre_activation)
    grad_activation = (cotangent.astype(jnp.float32) * gate_value * (1.0 + pre_activation * (1.0 - gate_value))).astype(jnp.bfloat16)
    grad_scale = 1.0 / math.sqrt(node_count)
    grad_self = jnp.dot(features.T, grad_activation, preferred_element_type=jnp.float32) * grad_scale
    grad_neighbor = jnp.dot(aggregate.T, grad_activation, preferred_element_type=jnp.float32) * grad_scale
    grad_bias = lax.optimization_barrier(jnp.sum(grad_activation.astype(jnp.float32), axis=0)) * grad_scale
    grad_aggregate = jnp.dot(grad_activation, neighbor_weight.T, preferred_element_type=jnp.float32).astype(jnp.bfloat16)
    self_grad = jnp.dot(grad_activation, self_weight.T, preferred_element_type=jnp.float32)
    grad_tiles = grad_aggregate.reshape(blocks, tile_rows, tile_size, feature_width)

    def spread_block(target, totals):

        def one_offset(offset, inner):
            source, tile_block, active = block_terms(target, offset)
            picked = grad_tiles[target][tile_target[target, offset]].astype(jnp.float32)
            products = jnp.einsum('jab,jaf->jbf', tile_block, picked, precision=highest)
            placer = jax.nn.one_hot(tile_source[target, offset], tile_rows, dtype=jnp.float32) * active[:, None]
            return inner.at[source].add(jnp.einsum('jt,jbf->tbf', placer, products, precision=highest))
        totals = lax.fori_loop(0, blocks, one_offset, totals)
        weights, hub_active, hub_rows = hub_terms(target)
        start = (target * rows_dev).astype(jnp.int32)
        reader_grad = lax.dynamic_slice_in_dim(grad_aggregate, start, rows_dev, 0).astype(jnp.float32)
        returned = jnp.einsum('sjn,nf->sjf', weights, reader_grad, precision=highest)
        returned = jnp.where(hub_active[:, :, None], returned, jnp.zeros((), jnp.float32))
        flat_grads = totals.reshape(node_count, feature_width).at[hub_rows.reshape(-1)].add(returned.reshape(-1, feature_width))
        return flat_grads.reshape(totals.shape)
    spread = lax.fori_loop(0, blocks, spread_block, jnp.zeros((blocks, tile_rows, tile_size, feature_width), jnp.float32))
    grad_input = (spread.reshape(node_count, feature_width) + self_grad).astype(jnp.bfloat16)
    return (output, grad_input, grad_self, grad_neighbor, grad_bias)
```

```python
import math

import jax
import jax.numpy as jnp
from jax import lax
from jax.experimental import pallas as pl
from jax.experimental.pallas import tpu as pltpu
from jax.sharding import PartitionSpec as P


AXES = ("blk", "rep")
COLS = 9
HEAD = 16


def route(source_of):
    pairs = []
    for block in range(64):
        for r in range(2):
            q, l, c = block // 4, (block // 2) % 2, block % 2
            q2, l2, c2, r2 = source_of(q, l, c, r)
            pairs.append(((((q2 % 16) * 2 + l2 % 2) * 2 + c2 % 2) * 2 + r2 % 2, block * 2 + r))
    return pairs


def inverse(pairs):
    return [(d, s) for s, d in pairs]


def y_source(q, l, c, r):
    y = (2 * r + l + (1 if c else -1)) % 4
    return (q, y % 2, c, y // 2)


SWAP_Y = route(y_source)
SWAP_L = route(lambda q, l, c, r: (q, l + 1, c, r))
SWAP_C = route(lambda q, l, c, r: (q, l, c + 1, r))
SWAP_R = route(lambda q, l, c, r: (q, l, c, r + 1))
FROM_COL = [route(lambda q, l, c, r, k=k: (q + (k if r else -k), l, c, r)) for k in range(5)]


def as_bf16(x):
    return lax.reduce_precision(x, 8, 7)


def permute(x, pairs):
    return lax.ppermute(x, AXES, pairs)


def slot_numbers(ids_ref, cls, k, lr):
    block, r = ids_ref[0], ids_ref[1]
    q = lax.bitwise_and(block // 4 + jnp.where(r == 1, k, -k) + 16, 15)
    low = lax.bitwise_xor(lax.bitwise_and(block, 3), lr * 2 + cls)
    source = q * 4 + low
    offset = lax.bitwise_and(block - source + 64, 63) - 32 * r
    valid = jnp.logical_and(offset >= 0, offset < 32)
    return source, jnp.where(valid, offset, 0), valid


def densify_kernel(count_ref, code_ref, tiles_ref, out_ref, acc_ref):
    step = pl.program_id(0)
    acc_ref[...] = jnp.zeros_like(acc_ref)

    def add(j, carry):
        code = code_ref[step * 16 + j]
        acc_ref[code] += tiles_ref[0, 0, j].astype(jnp.float32)
        return carry

    lax.fori_loop(0, count_ref[step], add, 0)
    for t in range(2):
        for s in range(2):
            out_ref[0, t * 128 : (t + 1) * 128, s * 128 : (s + 1) * 128] = acc_ref[
                t * 2 + s
            ].astype(jnp.bfloat16)


def densify(tile_values, tile_target, tile_source, tile_count):
    offsets, slots = tile_target.shape[1:]
    code = (tile_target[0] * 2 + tile_source[0]).reshape(-1)
    return pl.pallas_call(
        densify_kernel,
        grid_spec=pltpu.PrefetchScalarGridSpec(
            num_scalar_prefetch=2,
            grid=(offsets,),
            in_specs=[pl.BlockSpec((1, 1, slots, 128, 128), lambda o, n, c: (0, o, 0, 0, 0))],
            out_specs=pl.BlockSpec((1, 256, 256), lambda o, n, c: (o, 0, 0)),
            scratch_shapes=[pltpu.VMEM((4, 128, 128), jnp.float32)],
        ),
        out_shape=jax.ShapeDtypeStruct((offsets, 256, 256), jnp.bfloat16),
        cost_estimate=pl.CostEstimate(
            flops=8 * 2**20, transcendentals=0, bytes_accessed=20 * 2**20
        ),
        name="densify",
    )(tile_count[0], code, tile_values)


def dot(a, b):
    return jnp.dot(a, b, preferred_element_type=jnp.float32)


def dot_tn(a, b):
    return lax.dot_general(a, b, (((0,), (0,)), ((), ())), preferred_element_type=jnp.float32)


def forward_kernel(ids_ref, *refs):
    own_a, own_b, own_c, oth_a, oth_c, mats_ref, hub_ref, out_ref, hot_ref, pick_ref, wts_ref = refs
    rows = 256 + HEAD
    out_ref[...] = jnp.zeros_like(out_ref)
    lane = lax.broadcasted_iota(jnp.int32, (HEAD, 128), 1)
    column = lax.broadcasted_iota(jnp.int32, (HEAD, 256), 1)

    def segment(ref, first, cls, k0, count):
        def body(i, carry):
            k = k0 + i // 2
            lr = lax.bitwise_and(i, 1)
            source, offset, valid = slot_numbers(ids_ref, cls, k, lr)
            base = pl.multiple_of((first * 2 + i) * rows, 16)
            slot = (cls * COLS + k) * 2 + lr
            at = pl.multiple_of(slot * HEAD, HEAD)
            block = ref[pl.ds(base, 256), :]
            head = ref[pl.ds(base + 256, HEAD), :].astype(jnp.float32)
            mine = jnp.sum(jnp.where(lane == ids_ref[0], head, 0.0), axis=1, keepdims=True)
            mine = jnp.where(valid, mine, -1.0).astype(jnp.int32)
            hot = (mine == column).astype(jnp.float32).astype(jnp.bfloat16)
            hot_ref[pl.ds(at, HEAD), :] = hot
            pick_ref[pl.ds(at, HEAD), :] = dot(hot, block).astype(jnp.bfloat16)
            wts_ref[pl.ds(at, HEAD), :] = hub_ref[source]

            @pl.when(valid)
            def _():
                out_ref[...] += dot(mats_ref[offset], block)

            return carry

        lax.fori_loop(0, 2 * count, body, 0)

    segment(own_a, 0, 0, 0, 1)
    segment(own_b, 0, 0, 1, 4)
    segment(own_c, 0, 0, 5, 4)
    segment(oth_a, 0, 1, 0, 5)
    segment(oth_c, 0, 1, 5, 4)
    out_ref[...] += dot_tn(wts_ref[...], pick_ref[...])


def vmem():
    return pl.BlockSpec(memory_space=pltpu.VMEM)


def smem():
    return pl.BlockSpec(memory_space=pltpu.SMEM)


def forward(ids, own_a, own_b, own_c, oth_a, oth_c, mats, hub):
    slots = 4 * COLS
    return pl.pallas_call(
        forward_kernel,
        in_specs=[smem()] + [vmem()] * 7,
        out_specs=[vmem(), vmem()],
        out_shape=[
            jax.ShapeDtypeStruct((256, 128), jnp.float32),
            jax.ShapeDtypeStruct((slots * HEAD, 256), jnp.bfloat16),
        ],
        scratch_shapes=[
            pltpu.VMEM((slots * HEAD, 128), jnp.bfloat16),
            pltpu.VMEM((slots * HEAD, 256), jnp.bfloat16),
        ],
        name="forward",
    )(ids, own_a, own_b, own_c, oth_a, oth_c, mats, hub)


def middle_kernel(
    ids_ref, mine_ref, theirs_ref, feat_ref, sw_ref, nw_ref, ct_ref, bias_ref, other_ref, *outs
):
    out_ref, grad_ref, self_ref, wgrad_ref = outs
    r = ids_ref[1]
    feats = feat_ref[...]
    agg = (mine_ref[...] + theirs_ref[...]).astype(jnp.bfloat16)

    def half(sw, nw, ct, bias):
        pre = dot(feats, sw) + dot(agg, nw) + bias
        gate = jax.nn.sigmoid(pre)
        act = ct.astype(jnp.float32) * gate * (1.0 + pre * (1.0 - gate))
        return pre * gate, act.astype(jnp.bfloat16)

    def dot_nt(a, b):
        return lax.dot_general(a, b, (((1,), (1,)), ((), ())), preferred_element_type=jnp.float32)

    sw, nw = sw_ref[...], nw_ref[...]
    sw2, nw2 = other_ref[0:128, :], other_ref[128:256, :]
    extra = other_ref[512:528, :].astype(jnp.float32)
    bias2 = extra[0:1] + extra[1:2] + extra[2:3]
    value, act = half(sw, nw, ct_ref[...], bias_ref[...])
    _, act2 = half(sw2, nw2, other_ref[256:512, :], bias2)
    out_ref[...] = value.astype(jnp.bfloat16)
    mine_g, theirs_g = dot_nt(act, nw), dot_nt(act2, nw2)
    grad_ref[...] = (mine_g + theirs_g).astype(jnp.bfloat16)
    self_ref[...] = dot_nt(act, sw) + dot_nt(act2, sw2)
    wgrad_ref[0:128, :] = dot_tn(feats, act)
    wgrad_ref[128:256, :] = dot_tn(agg, act)
    wgrad_ref[256:320, :] = jnp.zeros((64, 128), jnp.float32)
    wgrad_ref[256:257, :] = jnp.sum(act.astype(jnp.float32), axis=0, keepdims=True)


def middle(ids, *args):
    return pl.pallas_call(
        middle_kernel,
        in_specs=[smem()] + [vmem()] * 8,
        out_specs=[vmem()] * 4,
        out_shape=[
            jax.ShapeDtypeStruct((256, 128), jnp.bfloat16),
            jax.ShapeDtypeStruct((256, 128), jnp.bfloat16),
            jax.ShapeDtypeStruct((256, 128), jnp.float32),
            jax.ShapeDtypeStruct((320, 128), jnp.float32),
        ],
        name="middle",
    )(ids, *args)


def backward_kernel(cls, ids_ref, grad_ref, mats_ref, hub_ref, hot_ref, out_ref):
    grad = grad_ref[...]

    def body(i, carry):
        source, offset, valid = slot_numbers(ids_ref, cls, i // 2, lax.bitwise_and(i, 1))
        at = pl.multiple_of((cls * COLS * 2 + i) * HEAD, HEAD)
        base = pl.multiple_of(i * 256, 256)

        @pl.when(valid)
        def _():
            back = dot(hub_ref[source], grad).astype(jnp.bfloat16)
            part = dot_tn(mats_ref[offset], grad) + dot_tn(hot_ref[pl.ds(at, HEAD), :], back)
            out_ref[pl.ds(base, 256), :] = part.astype(out_ref.dtype)

        @pl.when(jnp.logical_not(valid))
        def _():
            out_ref[pl.ds(base, 256), :] = jnp.zeros((256, 128), out_ref.dtype)

        return carry

    lax.fori_loop(0, 2 * COLS, body, 0)


def backward(cls, dtype, ids, grad, mats, hub, hot):
    def kernel(*refs):
        backward_kernel(cls, *refs)

    return pl.pallas_call(
        kernel,
        in_specs=[smem()] + [vmem()] * 4,
        out_specs=vmem(),
        out_shape=jax.ShapeDtypeStruct((COLS * 512, 128), dtype),
        name="backward_%d" % cls,
    )(ids, grad, mats, hub, hot)


def on_device(
    features,
    tile_values,
    tile_target,
    tile_source,
    tile_count,
    hub_list,
    hub_count,
    hub_weight,
    self_weight,
    neighbor_weight,
    bias,
    cotangent,
):
    f32, bf16 = jnp.float32, jnp.bfloat16
    blocks = lax.axis_size("blk")
    ids = jnp.stack([lax.axis_index("blk"), lax.axis_index("rep")]).astype(jnp.int32)

    live = jnp.arange(HEAD, dtype=jnp.int32)[None, :] < hub_count[0][:, None]
    lists = jnp.where(live, hub_list[0], -1).astype(bf16).T
    lists = jnp.pad(lists, ((0, 0), (0, 128 - blocks)), constant_values=-1)
    block = jnp.concatenate([features, lists], axis=0)

    col0 = jnp.concatenate([block, permute(block, SWAP_Y)], axis=0)
    bias_hi = as_bf16(bias)
    bias_mid = as_bf16(bias - bias_hi)
    bias_lo = bias - bias_hi - bias_mid
    bias_rows = jnp.stack([bias_hi, bias_mid, bias_lo]).astype(bf16)
    bias_rows = jnp.pad(bias_rows, ((0, 13), (0, 0)))
    packed = jnp.concatenate([self_weight, neighbor_weight, cotangent, bias_rows], axis=0)
    other = permute(packed, SWAP_R)

    cols = jnp.concatenate([permute(col0, FROM_COL[k]) for k in range(1, 5)], axis=0)
    far = permute(cols, FROM_COL[4])
    oth_near = permute(jnp.concatenate([col0, cols], axis=0), SWAP_C)
    mats = densify(tile_values, tile_target, tile_source, tile_count)
    oth_far = permute(far, SWAP_C)
    partial, hot = forward(ids, col0, cols, far, oth_near, oth_far, mats, hub_weight)
    theirs = permute(partial, SWAP_R)
    output, grad, self_grad, wgrad = middle(
        ids,
        partial,
        theirs,
        features,
        self_weight,
        neighbor_weight,
        cotangent,
        bias[None, :],
        other,
    )

    give = backward(1, bf16, ids, grad, mats, hub_weight, hot)
    got = permute(give, SWAP_C)
    keep = backward(0, f32, ids, grad, mats, hub_weight, hot)
    got_far = permute((keep[5 * 512 :] + got[5 * 512 :].astype(f32)).astype(bf16), inverse(FROM_COL[4]))

    scale = 1.0 / math.sqrt(256 * blocks)
    pieces = lax.all_to_all(wgrad.reshape(blocks, 5, 128), "blk", 0, 0, tiled=True)
    summed = jnp.sum(pieces, axis=0, keepdims=True) * scale
    whole = lax.all_to_all(
        jnp.broadcast_to(summed, (blocks, 5, 128)), "blk", 0, 0, tiled=True
    ).reshape(320, 128)

    near = keep[512 : 5 * 512] + got[512 : 5 * 512].astype(f32) + got_far.astype(f32)
    near = near.astype(bf16)
    mine = keep[:512] + got[:512].astype(f32)
    for k in range(1, 5):
        mine += permute(near[(k - 1) * 512 : k * 512], inverse(FROM_COL[k])).astype(f32)
    total = mine[:256] + permute(mine[256:].astype(bf16), SWAP_L).astype(f32)
    total = as_bf16(total)
    theirs = permute(total.astype(bf16), SWAP_R)
    grad_input = total + theirs.astype(f32) + self_grad
    return (
        output,
        grad_input.astype(bf16),
        whole[:128],
        whole[128:256],
        whole[256],
    )


def solution(mesh):
    in_specs = (
        P("blk", None),
        P("blk", "rep", None, None, None),
        P("blk", "rep", None),
        P("blk", "rep", None),
        P("blk", "rep"),
        P("blk", None, None),
        P("blk", None),
        P(None, None, "blk"),
        P(None, "rep"),
        P(None, "rep"),
        P("rep"),
        P("blk", "rep"),
    )
    out_specs = (P("blk", "rep"), P("blk", None), P(None, "rep"), P(None, "rep"), P("rep"))
    return jax.shard_map(
        on_device, mesh=mesh, in_specs=in_specs, out_specs=out_specs, check_vma=False
    )
```

```python
import functools
import math

import jax
import jax.numpy as jnp
from jax import lax
from jax.experimental import pallas as pl
from jax.experimental.pallas import tpu as pltpu
from jax.sharding import PartitionSpec as P


AXES = ("blk", "rep")
COLS = 9
SLOTS = 4 * COLS
HEAD = 16
GROUP = 2 * (256 + HEAD)
BACK = 128 + 8
MIB = 2**20


def route(source_of):
    pairs = []
    for block in range(64):
        for r in range(2):
            q, l, c = block // 4, (block // 2) % 2, block % 2
            q2, l2, c2, r2 = source_of(q, l, c, r)
            pairs.append(((((q2 % 16) * 2 + l2 % 2) * 2 + c2 % 2) * 2 + r2 % 2, block * 2 + r))
    return pairs


def inverse(pairs):
    return [(d, s) for s, d in pairs]


def y_step(step):
    def source(q, l, c, r):
        y = (2 * r + l + step(c)) % 4
        return (q, y % 2, c, y // 2)

    return route(source)


SWAP_Y = y_step(lambda c: 1 if c else -1)
FROM_DOWN = y_step(lambda c: -1)
FROM_UP = y_step(lambda c: 1)
SWAP_C = route(lambda q, l, c, r: (q, l, c + 1, r))
SWAP_R = route(lambda q, l, c, r: (q, l, c, r + 1))
FROM_COL = [route(lambda q, l, c, r, k=k: (q + (k if r else -k), l, c, r)) for k in range(5)]


def permute(x, pairs):
    return lax.ppermute(x, AXES, pairs)


def as_bf16(x):
    return lax.reduce_precision(x, 8, 7)


def dot(a, b):
    return jnp.dot(a, b, preferred_element_type=jnp.float32)


def dot_nt(a, b):
    return lax.dot_general(a, b, (((1,), (1,)), ((), ())), preferred_element_type=jnp.float32)


def dot_tn(a, b):
    return lax.dot_general(a, b, (((0,), (0,)), ((), ())), preferred_element_type=jnp.float32)


def slot_source(ids_ref, cls, k, lr):
    block, r = ids_ref[0], ids_ref[1]
    q = lax.bitwise_and(block // 4 + jnp.where(r == 1, k, -k) + 16, 15)
    source = q * 4 + lax.bitwise_xor(lax.bitwise_and(block, 3), lr * 2 + cls)
    offset = lax.bitwise_and(block - source + 64, 63) - 32 * r
    return source, jnp.logical_and(offset >= 0, offset < 32)


def offset_slot(ids_ref, offset):
    block, r = ids_ref[0], ids_ref[1]
    source = lax.bitwise_and(block - offset - 32 * r + 128, 63)
    k = lax.bitwise_and((block // 4 - source // 4) * jnp.where(r == 1, -1, 1) + 16, 15)
    differ = lax.bitwise_xor(lax.bitwise_and(block, 3), lax.bitwise_and(source, 3))
    return (lax.bitwise_and(differ, 1) * COLS + k) * 2 + differ // 2


def vmem():
    return pl.BlockSpec(memory_space=pltpu.VMEM)


def smem():
    return pl.BlockSpec(memory_space=pltpu.SMEM)


def kernel_call(body, n_in, outs, scratch=(), limit=8 * MIB):
    single = not isinstance(outs, list)
    shapes = [jax.ShapeDtypeStruct(*o) for o in ([outs] if single else outs)]

    def call(*args):
        return pl.pallas_call(
            body,
            in_specs=[smem()] + [vmem()] * n_in,
            out_specs=vmem() if single else [vmem()] * len(shapes),
            out_shape=shapes[0] if single else shapes,
            scratch_shapes=list(scratch),
            compiler_params=pltpu.CompilerParams(vmem_limit_bytes=limit),
        )(*args)

    return call


STEP = 4


def densify_kernel(ids_ref, count_ref, code_ref, tiles_ref, out_ref, acc_ref):
    step = pl.program_id(0)

    @pl.when(step == 0)
    def _():
        for cls in range(2):
            for k in (0, COLS - 1):
                for lr in range(2):
                    _, valid = slot_source(ids_ref, cls, k, lr)

                    @pl.when(jnp.logical_not(valid))
                    def _():
                        out_ref[(cls * COLS + k) * 2 + lr] = jnp.zeros((256, 256), jnp.bfloat16)

    for u in range(STEP):
        offset = step * STEP + u
        acc_ref[...] = jnp.zeros_like(acc_ref)

        def add(j, carry):
            code = code_ref[offset * 16 + j]
            acc_ref[code] += tiles_ref[0, u, j].astype(jnp.float32)
            return carry

        lax.fori_loop(0, count_ref[offset], add, 0)
        slot = offset_slot(ids_ref, offset)
        for t in range(2):
            for s in range(2):
                out_ref[slot, t * 128 : (t + 1) * 128, s * 128 : (s + 1) * 128] = acc_ref[
                    t * 2 + s
                ].astype(jnp.bfloat16)


def densify(ids, tile_values, tile_target, tile_source, tile_count):
    offsets, slots = tile_target.shape[1:]
    code = (tile_target[0] * 2 + tile_source[0]).reshape(-1)
    return pl.pallas_call(
        densify_kernel,
        grid_spec=pltpu.PrefetchScalarGridSpec(
            num_scalar_prefetch=3,
            grid=(offsets // STEP,),
            in_specs=[pl.BlockSpec((1, STEP, slots, 128, 128), lambda o, i, n, c: (0, o, 0, 0, 0))],
            out_specs=pl.BlockSpec((SLOTS, 256, 256), lambda o, i, n, c: (0, 0, 0)),
            scratch_shapes=[pltpu.VMEM((4, 128, 128), jnp.float32)],
        ),
        out_shape=jax.ShapeDtypeStruct((SLOTS, 256, 256), jnp.bfloat16),
        compiler_params=pltpu.CompilerParams(vmem_limit_bytes=20 * MIB),
        name="densify",
    )(ids, tile_count[0], code, tile_values)


def forward_kernel(ids_ref, *refs):
    groups, (mats_ref, hub_ref, out_ref, hot_ref, pick_ref, wts_ref) = refs[:6], refs[6:]
    lane = lax.broadcasted_iota(jnp.int32, (2 * HEAD, 128), 1)
    column = lax.broadcasted_iota(jnp.int32, (2 * HEAD, 256), 1)
    total = None
    for cls in range(2):
        for k in range(COLS):
            part = 0 if k == 0 else (1 if k < 5 else 2)
            ref, base = groups[cls * 3 + part], (0 if k == 0 else (k - 1) % 4) * GROUP
            head = ref[base + 512 : base + GROUP, :].astype(jnp.float32)
            mine = jnp.sum(jnp.where(lane == ids_ref[0], head, 0.0), axis=1, keepdims=True)
            hot = (mine.astype(jnp.int32) == column).astype(jnp.float32).astype(jnp.bfloat16)
            for lr in range(2):
                slot = (cls * COLS + k) * 2 + lr
                source, valid = slot_source(ids_ref, cls, k, lr)
                at = slice(slot * HEAD, (slot + 1) * HEAD)
                one = hot[lr * HEAD : (lr + 1) * HEAD, :]
                block = ref[base + lr * 256 : base + (lr + 1) * 256, :]
                both = dot(jnp.concatenate([mats_ref[slot], one], axis=0), block)
                total = both[:256] if total is None else total + both[:256]
                hot_ref[at, :] = one
                pick_ref[at, :] = both[256:].astype(jnp.bfloat16)
                weights = hub_ref[source]
                wts_ref[at, :] = jnp.where(valid, weights, jnp.zeros_like(weights))
    out_ref[...] = total + dot_tn(wts_ref[...], pick_ref[...])


def forward(*args):
    return kernel_call(
        forward_kernel,
        8,
        [
            ((256, 128), jnp.float32),
            ((SLOTS * HEAD, 256), jnp.bfloat16),
            ((SLOTS * HEAD, 128), jnp.bfloat16),
            ((SLOTS * HEAD, 256), jnp.bfloat16),
        ],
        limit=24 * MIB,
    )(*args)


def middle_kernel(
    ids_ref, mine_ref, theirs_ref, feat_ref, sw_ref, nw_ref, ct_ref, bias_ref, other_ref, *outs
):
    out_ref, grad_ref, self_ref, wgrad_ref, bgrad_ref = outs
    first = ids_ref[1] == 0
    feats = feat_ref[...]
    agg = (mine_ref[...] + theirs_ref[...]).astype(jnp.bfloat16)

    def half(sw, nw, ct, bias):
        pre = dot(feats, sw) + dot(agg, nw) + bias
        gate = jax.nn.sigmoid(pre)
        act = ct.astype(jnp.float32) * gate * (1.0 + pre * (1.0 - gate))
        return pre * gate, act.astype(jnp.bfloat16)

    sw, nw = sw_ref[...], nw_ref[...]
    sw2, nw2 = other_ref[0:128, :], other_ref[128:256, :]
    extra = other_ref[512:528, :].astype(jnp.float32)
    bias2 = extra[0:1] + extra[1:2] + extra[2:3]
    value, act = half(sw, nw, ct_ref[...], bias_ref[...])
    _, act2 = half(sw2, nw2, other_ref[256:512, :], bias2)
    out_ref[...] = value.astype(jnp.bfloat16)
    grad_ref[...] = (dot_nt(nw, act) + dot_nt(nw2, act2)).astype(jnp.bfloat16)
    self_ref[...] = dot_nt(sw, act) + dot_nt(sw2, act2)
    bgrad_ref[...] = jnp.zeros_like(bgrad_ref)
    for h in range(2):
        now = jnp.where(first, act2, act) if h else jnp.where(first, act, act2)
        wgrad_ref[h * 256 : h * 256 + 128, :] = dot_tn(now, feats)
        wgrad_ref[h * 256 + 128 : h * 256 + 256, :] = dot_tn(now, agg)
        bgrad_ref[h : h + 1, :] = jnp.sum(now.astype(jnp.float32), axis=0, keepdims=True)


def middle(*args):
    return kernel_call(
        middle_kernel,
        8,
        [
            ((256, 128), jnp.bfloat16),
            ((128, 256), jnp.bfloat16),
            ((128, 256), jnp.float32),
            ((512, 128), jnp.float32),
            ((8, 128), jnp.float32),
        ],
    )(*args)


def backward_kernel(cls, columns, add, ids_ref, grad_ref, mats_ref, wts_ref, hot_ref, wg_ref, bg_ref, *refs):
    out_ref = refs[-1]
    grad = grad_ref[...]
    for i, k in enumerate(columns):
        for lr in range(2):
            slot = (cls * COLS + k) * 2 + lr
            at = slice(slot * HEAD, (slot + 1) * HEAD)
            lanes = slice(lr * 256, (lr + 1) * 256)
            source, valid = slot_source(ids_ref, cls, k, lr)
            back = dot_nt(grad, wts_ref[at, :]).astype(jnp.bfloat16)
            part = dot(grad, mats_ref[slot]) + dot(back, hot_ref[at, :])
            chunk = wg_ref[pl.ds(pl.multiple_of(source * 8, 8), 8), :]
            chunk = jnp.concatenate([chunk, bg_ref[...]], axis=1)
            chunk = jnp.where(valid, chunk, 0.0)
            if add:
                part += refs[0][i, 0:128, lanes].astype(jnp.float32)
                chunk += refs[0][i, 128:BACK, lanes].astype(jnp.float32)
            out_ref[i, 0:128, lanes] = part.astype(out_ref.dtype)
            out_ref[i, 128:BACK, lanes] = chunk.astype(out_ref.dtype)


def backward(cls, columns, dtype, ids, args, got=None):
    body = functools.partial(backward_kernel, cls, columns, got is not None)
    more = () if got is None else (got,)
    shape = (len(columns), BACK, 512)
    return kernel_call(body, 6 + len(more), (shape, dtype), limit=20 * MIB)(ids, *args, *more)


def near_kernel(ids_ref, keep_ref, far_ref, *outs):
    for i, out in enumerate(outs):
        out[...] = (keep_ref[i + 1] + far_ref[i].astype(jnp.float32)).astype(jnp.bfloat16)


def mine_kernel(ids_ref, keep_ref, *refs):
    got, (same_ref, cross_ref) = refs[:4], refs[4:]
    total = keep_ref[0]
    for ref in got:
        total += ref[...].astype(jnp.float32)
    same_ref[...] = total[:, :256].astype(jnp.bfloat16)
    cross_ref[...] = total[:, 256:].astype(jnp.bfloat16)


def finish_kernel(ids_ref, same_ref, rep_ref, down_ref, up_ref, self_ref, grad_ref, pay_ref):
    f32 = jnp.float32
    total = (same_ref[...].astype(f32) + rep_ref[...].astype(f32)) + (
        down_ref[...].astype(f32) + up_ref[...].astype(f32)
    )
    grad_ref[...] = (total[:128] + self_ref[...]).T.astype(jnp.bfloat16)
    useful = ids_ref[0] // 32 == ids_ref[1]
    pay = jnp.where(useful, total[128:, :128], total[128:, 128:])
    pay_ref[...] = jnp.broadcast_to(pay[None], pay_ref.shape)


def weights_kernel(scale, ids_ref, got_ref, self_ref, neighbor_ref, bias_ref):
    r = ids_ref[1]
    start = pl.multiple_of(r * 256, 256)
    self_ref[...] = got_ref[pl.ds(start, 128), :].T * scale
    neighbor_ref[...] = got_ref[pl.ds(start + 128, 128), :].T * scale
    rows = got_ref[pl.ds(pl.multiple_of(256 - start, 256), 8), :]
    row = lax.broadcasted_iota(jnp.int32, rows.shape, 0)
    bias_ref[...] = jnp.sum(jnp.where(row == r, rows, 0.0), axis=0, keepdims=True) * scale


def layer(
    features,
    tile_values,
    tile_target,
    tile_source,
    tile_count,
    hub_list,
    hub_count,
    hub_weight,
    self_weight,
    neighbor_weight,
    bias,
    cotangent,
):
    f32, bf16 = jnp.float32, jnp.bfloat16
    blocks = lax.axis_size("blk")
    ids = jnp.stack([lax.axis_index("blk"), lax.axis_index("rep")]).astype(jnp.int32)

    live = jnp.arange(HEAD, dtype=jnp.int32)[None, :] < hub_count[0][:, None]
    lists = jnp.where(live, hub_list[0], -1).astype(bf16).T
    lists = jnp.pad(lists, ((0, 0), (0, 128 - blocks)), constant_values=-1)
    block = jnp.concatenate([features, lists], axis=0)
    theirs = permute(block, SWAP_Y)

    bias_hi = as_bf16(bias)
    bias_mid = as_bf16(bias - bias_hi)
    bias_lo = bias - bias_hi - bias_mid
    bias_rows = jnp.stack([bias_hi, bias_mid, bias_lo]).astype(bf16)
    bias_rows = jnp.pad(bias_rows, ((0, 13), (0, 0)))
    packed = jnp.concatenate([self_weight, neighbor_weight, cotangent, bias_rows], axis=0)
    other = permute(packed, SWAP_R)

    col0 = jnp.concatenate([features, theirs[:256], lists, theirs[256:]], axis=0)
    cols = [permute(col0, FROM_COL[k]) for k in range(1, 5)]
    oth0 = permute(col0, SWAP_C)
    cols = jnp.concatenate(cols, axis=0)
    far = permute(cols, FROM_COL[4])
    oth1 = permute(cols, SWAP_C)
    mats = densify(ids, tile_values, tile_target, tile_source, tile_count)
    oth2 = permute(far, SWAP_C)

    partial, hot, _, wts = forward(ids, col0, cols, far, oth0, oth1, oth2, mats, hub_weight)
    theirs = permute(partial, SWAP_R)
    output, grad, self_grad, wgrad, bgrad = middle(
        ids,
        partial,
        theirs,
        features,
        self_weight,
        neighbor_weight,
        cotangent,
        bias[None, :],
        other,
    )

    shared = (grad, mats, wts, hot, wgrad, bgrad)
    near_cols, far_cols = tuple(range(5)), tuple(range(5, 9))
    got_far = permute(backward(1, far_cols, bf16, ids, shared), SWAP_C)
    got_near = permute(backward(1, near_cols, bf16, ids, shared), SWAP_C)
    sent = backward(0, far_cols, bf16, ids, shared, got_far)
    far_sums = permute(sent, inverse(FROM_COL[4]))
    keep = backward(0, near_cols, f32, ids, shared, got_near)
    piece = ((BACK, 512), bf16)
    near = kernel_call(near_kernel, 2, [piece] * 4)(ids, keep, far_sums)
    got = [permute(near[k - 1], inverse(FROM_COL[k])) for k in range(1, 5)]
    piece = ((BACK, 256), bf16)
    same, cross = kernel_call(mine_kernel, 5, [piece] * 2)(ids, keep, *got)
    over = permute(same, SWAP_R)
    down = permute(cross, FROM_DOWN)
    up = permute(cross, FROM_UP)
    grad_input, pay = kernel_call(
        finish_kernel, 5, [((256, 128), bf16), ((blocks, 8, 128), f32)]
    )(ids, same, over, down, up, self_grad)
    whole = lax.all_to_all(pay, "blk", 0, 0, tiled=True).reshape(blocks * 8, 128)
    scale = 1.0 / math.sqrt(256 * blocks)
    grad_self, grad_neighbor, grad_bias = kernel_call(
        functools.partial(weights_kernel, scale),
        1,
        [((128, 128), f32), ((128, 128), f32), ((1, 128), f32)],
    )(ids, whole)
    return output, grad_input, grad_self, grad_neighbor, grad_bias[0]


def solution(mesh):
    in_specs = (
        P("blk", None),
        P("blk", "rep", None, None, None),
        P("blk", "rep", None),
        P("blk", "rep", None),
        P("blk", "rep"),
        P("blk", None, None),
        P("blk", None),
        P(None, None, "blk"),
        P(None, "rep"),
        P(None, "rep"),
        P("rep"),
        P("blk", "rep"),
    )
    out_specs = (P("blk", "rep"), P("blk", None), P(None, "rep"), P(None, "rep"), P("rep"))
    return jax.shard_map(layer, mesh=mesh, in_specs=in_specs, out_specs=out_specs, check_vma=False)
```

```python
import functools
import math

import jax
import jax.numpy as jnp
from jax import lax
from jax.experimental import pallas as pl
from jax.experimental.pallas import tpu as pltpu
from jax.sharding import PartitionSpec as P


AXES = ("blk", "rep")
COLS = 9
HEAD = 16
PART = 64 + 8
GROUP = 2 * (256 + HEAD)
MIB = 2**20


def route(source_of):
    pairs = []
    for block in range(64):
        for r in range(2):
            q, l, c = block // 4, (block // 2) % 2, block % 2
            q2, l2, c2, r2 = source_of(q, l, c, r)
            pairs.append(((((q2 % 16) * 2 + l2 % 2) * 2 + c2 % 2) * 2 + r2 % 2, block * 2 + r))
    return pairs


def inverse(pairs):
    return [(d, s) for s, d in pairs]


def y_step(step):
    def source(q, l, c, r):
        y = (2 * r + l + step(c)) % 4
        return (q, y % 2, c, y // 2)

    return route(source)


SWAP_Y = y_step(lambda c: 1 if c else -1)
FROM_DOWN = y_step(lambda c: -1)
FROM_UP = y_step(lambda c: 1)
SWAP_C = route(lambda q, l, c, r: (q, l, c + 1, r))
SWAP_L = route(lambda q, l, c, r: (q, l + 1, c, r))
SWAP_R = route(lambda q, l, c, r: (q, l, c, r + 1))
SAME_X, SAME_Z = (
    [route(lambda q, l, c, r, m=m: (q ^ m, l, c, r)) for m in masks]
    for masks in ((1, 3, 2), (4, 12, 8))
)
FROM_COL = [route(lambda q, l, c, r, k=k: (q + (k if r else -k), l, c, r)) for k in range(5)]


def permute(x, pairs):
    return lax.ppermute(x, AXES, pairs)


def as_bf16(x):
    return lax.reduce_precision(x, 8, 7)


def dot(a, b):
    return jnp.dot(a, b, preferred_element_type=jnp.float32)


def dot_nt(a, b):
    return lax.dot_general(a, b, (((1,), (1,)), ((), ())), preferred_element_type=jnp.float32)


def dot_tn(a, b):
    return lax.dot_general(a, b, (((0,), (0,)), ((), ())), preferred_element_type=jnp.float32)


def slot_source(ids_ref, cls, k, lr):
    block, r = ids_ref[0], ids_ref[1]
    q = lax.bitwise_and(block // 4 + jnp.where(r == 1, k, -k) + 16, 15)
    source = q * 4 + lax.bitwise_xor(lax.bitwise_and(block, 3), lr * 2 + cls)
    offset = lax.bitwise_and(block - source + 64, 63) - 32 * r
    return source, jnp.logical_and(offset >= 0, offset < 32)


def vmem():
    return pl.BlockSpec(memory_space=pltpu.VMEM)


def smem():
    return pl.BlockSpec(memory_space=pltpu.SMEM)


def kernel_call(body, n_in, outs, scratch=(), limit=8 * MIB):
    single = not isinstance(outs, list)
    shapes = [jax.ShapeDtypeStruct(*o) for o in ([outs] if single else outs)]

    def call(*args):
        return pl.pallas_call(
            body,
            in_specs=[smem()] + [vmem()] * n_in,
            out_specs=vmem() if single else [vmem()] * len(shapes),
            out_shape=shapes[0] if single else shapes,
            scratch_shapes=list(scratch),
            compiler_params=pltpu.CompilerParams(vmem_limit_bytes=limit),
        )(*args)

    return call


DEPTH = 8
NEAR, FAR = tuple(range(5)), tuple(range(5, COLS))


def densify_kernel(columns, ids_ref, table_ref, tiles_ref, out_ref, *scratch):
    acc_ref, buf_ref, sem_ref = scratch
    slots = 4 * len(columns)
    counts_at, width = tiles_ref.shape[1] * tiles_ref.shape[2], tiles_ref.shape[2]

    def place(slot):
        cls = slot // (2 * len(columns))
        k = columns[0] + lax.rem(slot // 2, len(columns))
        source, valid = slot_source(ids_ref, cls, k, lax.rem(slot, 2))
        offset = lax.bitwise_and(ids_ref[0] - source + 64, 63) - 32 * ids_ref[1]
        return jnp.where(valid, offset, 0), valid

    def fetch(slot, at):
        offset, _ = place(slot)
        return pltpu.make_async_copy(tiles_ref.at[0, offset], buf_ref.at[at], sem_ref.at[at])

    for u in range(DEPTH):
        fetch(u, u).start()

    def body(slot, carry):
        at = lax.rem(slot, DEPTH)
        offset, valid = place(slot)
        acc_ref[...] = jnp.zeros_like(acc_ref)
        fetch(slot, at).wait()

        def add(j, inner):
            code = table_ref[offset * width + j]
            acc_ref[code] += buf_ref[at, j].astype(jnp.float32)
            return inner

        lax.fori_loop(0, jnp.where(valid, table_ref[counts_at + offset], 0), add, 0)

        @pl.when(slot + DEPTH < slots)
        def _():
            fetch(slot + DEPTH, at).start()

        for t in range(2):
            for s in range(2):
                out_ref[slot, t * 128 : (t + 1) * 128, s * 128 : (s + 1) * 128] = acc_ref[
                    t * 2 + s
                ].astype(jnp.bfloat16)
        return carry

    lax.fori_loop(0, slots, body, 0)


def densify(columns, ids, table, tile_values):
    return pl.pallas_call(
        functools.partial(densify_kernel, columns),
        in_specs=[smem()] * 2 + [pl.BlockSpec(memory_space=pltpu.HBM)],
        out_specs=vmem(),
        scratch_shapes=[
            pltpu.VMEM((4, 128, 128), jnp.float32),
            pltpu.VMEM((DEPTH,) + tile_values.shape[2:], jnp.bfloat16),
            pltpu.SemaphoreType.DMA((DEPTH,)),
        ],
        out_shape=jax.ShapeDtypeStruct((4 * len(columns), 256, 256), jnp.bfloat16),
        compiler_params=pltpu.CompilerParams(vmem_limit_bytes=48 * MIB),
    )(ids, table, tile_values)


def forward_kernel(columns, first, ids_ref, *refs):
    groups, (mats_ref, hub_ref), refs = refs[: 4 if first else 2], refs[4 if first else 2 :][:2], refs[6 if first else 4 :]
    before_ref, (out_ref, hot_ref, wts_ref, pick_ref) = (None, refs) if first else (refs[0], refs[1:])
    lane = lax.broadcasted_iota(jnp.int32, (2 * HEAD, 128), 1)
    column = lax.broadcasted_iota(jnp.int32, (2 * HEAD, 256), 1)
    total = None if first else before_ref[...]
    for cls in range(2):
        for i, k in enumerate(columns):
            if first:
                ref, base = groups[cls * 2 + min(k, 1)], max(k - 1, 0) * GROUP
            else:
                ref, base = groups[cls], i * GROUP
            head = ref[base + 512 : base + GROUP, :].astype(jnp.float32)
            mine = jnp.sum(jnp.where(lane == ids_ref[0], head, 0.0), axis=1, keepdims=True)
            hot = (mine.astype(jnp.int32) == column).astype(jnp.float32).astype(jnp.bfloat16)
            for lr in range(2):
                slot = (cls * len(columns) + i) * 2 + lr
                source, valid = slot_source(ids_ref, cls, k, lr)
                at = slice(slot * HEAD, (slot + 1) * HEAD)
                one = hot[lr * HEAD : (lr + 1) * HEAD, :]
                block = ref[base + lr * 256 : base + (lr + 1) * 256, :]
                both = dot(jnp.concatenate([mats_ref[slot], one], axis=0), block)
                total = both[:256] if total is None else total + both[:256]
                hot_ref[at, :] = one
                pick_ref[at, :] = both[256:].astype(jnp.bfloat16)
                weights = hub_ref[source]
                wts_ref[at, :] = jnp.where(valid, weights, jnp.zeros_like(weights))
    out_ref[...] = (total + dot_tn(wts_ref[...], pick_ref[...])).astype(out_ref.dtype)


def forward(columns, first, *args):
    rows = 4 * len(columns) * HEAD
    return kernel_call(
        functools.partial(forward_kernel, columns, first),
        len(args) - 1,
        [
            ((256, 128), jnp.float32 if first else jnp.bfloat16),
            ((rows, 256), jnp.bfloat16),
            ((rows, 256), jnp.bfloat16),
        ],
        scratch=[pltpu.VMEM((rows, 128), jnp.bfloat16)],
        limit=20 * MIB,
    )(*args)


def middle_kernel(
    ids_ref, mine_ref, theirs_ref, feat_ref, sw_ref, nw_ref, ct_ref, bias_ref, other_ref, *outs
):
    out_ref, grad_ref, self_ref, keep_ref, give_ref, sums_ref = outs
    feats = feat_ref[...]
    agg = mine_ref[...].astype(jnp.float32) + theirs_ref[...].astype(jnp.float32)
    agg = agg.astype(jnp.bfloat16)

    def half(sw, nw, ct, bias):
        pre = dot(feats, sw) + dot(agg, nw) + bias
        gate = jax.nn.sigmoid(pre)
        act = ct.astype(jnp.float32) * gate * (1.0 + pre * (1.0 - gate))
        return pre * gate, act.astype(jnp.bfloat16)

    sw, nw = sw_ref[...], nw_ref[...]
    sw2, nw2 = other_ref[0:128, :], other_ref[128:256, :]
    extra = other_ref[512:528, :].astype(jnp.float32)
    bias2 = extra[0:1] + extra[1:2] + extra[2:3]
    value, act = half(sw, nw, ct_ref[...], bias_ref[...])
    _, act2 = half(sw2, nw2, other_ref[256:512, :], bias2)
    out_ref[...] = value.astype(jnp.bfloat16)
    grad_ref[...] = (dot_nt(nw, act) + dot_nt(nw2, act2)).astype(jnp.bfloat16)
    self_ref[...] = dot_nt(sw, act) + dot_nt(sw2, act2)
    sums_ref[0:128, :] = dot_tn(act, feats)
    sums_ref[128:256, :] = dot_tn(act, agg)
    bias_sum = jnp.sum(act.astype(jnp.float32), axis=0, keepdims=True)
    low = lax.bitwise_and(ids_ref[0], 3)
    for lr in range(2):
        for cls, ref in enumerate((keep_ref, give_ref)):
            quarter = lax.bitwise_xor(low, 2 * lr + cls)
            ref[lr, 0:64, :] = sums_ref[pl.ds(pl.multiple_of(quarter * 64, 64), 64), :]
            ref[lr, 64:PART, :] = jnp.broadcast_to(bias_sum, (PART - 64, 128))


def middle(*args):
    return kernel_call(
        middle_kernel,
        8,
        [
            ((256, 128), jnp.bfloat16),
            ((128, 256), jnp.bfloat16),
            ((128, 256), jnp.float32),
            ((2, PART, 128), jnp.float32),
            ((2, PART, 128), jnp.float32),
        ],
        scratch=[pltpu.VMEM((256, 128), jnp.float32)],
    )(*args)


def backward_kernel(cls, columns, add, ids_ref, grad_ref, mats_ref, hot_ref, wts_ref, *refs):
    out_ref = refs[-1]
    grad = grad_ref[...]
    for i in range(len(columns)):
        for lr in range(2):
            slot = (cls * len(columns) + i) * 2 + lr
            at = slice(slot * HEAD, (slot + 1) * HEAD)
            lanes = slice(lr * 256, (lr + 1) * 256)
            back = dot_nt(grad, wts_ref[at, :]).astype(jnp.bfloat16)
            part = dot(grad, mats_ref[slot]) + dot(back, hot_ref[at, :])
            if add:
                part += refs[0][i, :, lanes].astype(jnp.float32)
            out_ref[i, :, lanes] = part.astype(out_ref.dtype)


def backward(cls, columns, dtype, *args):
    body = functools.partial(backward_kernel, cls, columns, len(args) > 5)
    return kernel_call(body, len(args) - 1, ((len(columns), 128, 512), dtype), limit=20 * MIB)(
        *args
    )


def near_kernel(ids_ref, keep_ref, far_ref, *outs):
    for i, out in enumerate(outs):
        out[...] = (keep_ref[i + 1] + far_ref[i].astype(jnp.float32)).astype(jnp.bfloat16)


def mine_kernel(ids_ref, keep_ref, *refs):
    got, (same_ref, cross_ref) = refs[:4], refs[4:]
    total = keep_ref[0]
    for ref in got:
        total += ref[...].astype(jnp.float32)
    same_ref[...] = total[:, :256].astype(jnp.bfloat16)
    cross_ref[...] = total[:, 256:].astype(jnp.bfloat16)


def finish_kernel(ids_ref, same_ref, rep_ref, down_ref, up_ref, self_ref, grad_ref):
    f32 = jnp.float32
    total = (same_ref[...].astype(f32) + rep_ref[...].astype(f32)) + (
        down_ref[...].astype(f32) + up_ref[...].astype(f32)
    )
    grad_ref[...] = (total + self_ref[...]).T.astype(jnp.bfloat16)


def weights_kernel(scale, ids_ref, mine_ref, line_ref, core_ref, *refs):
    self_ref, neighbor_ref, bias_ref, sums_ref, bias_sums_ref = refs
    low = lax.bitwise_and(ids_ref[0], 3)
    for lr in range(2):
        for cls in range(2):
            part = core_ref.at[lr] if cls else (line_ref if lr else mine_ref)
            quarter = lax.bitwise_xor(low, 2 * lr + cls)
            sums_ref[pl.ds(pl.multiple_of(quarter * 64, 64), 64), :] = part[0:64, :]
            bias_sums_ref[quarter] = part[64:PART, :]
    self_ref[...] = sums_ref[0:128, :].T * scale
    neighbor_ref[...] = sums_ref[128:256, :].T * scale
    bias_ref[...] = bias_sums_ref[0][0:1] * scale


def layer(
    features,
    tile_values,
    tile_target,
    tile_source,
    tile_count,
    hub_list,
    hub_count,
    hub_weight,
    self_weight,
    neighbor_weight,
    bias,
    cotangent,
):
    f32, bf16 = jnp.float32, jnp.bfloat16
    blocks = lax.axis_size("blk")
    ids = jnp.stack([lax.axis_index("blk"), lax.axis_index("rep")]).astype(jnp.int32)

    live = jnp.arange(HEAD, dtype=jnp.int32)[None, :] < hub_count[0][:, None]
    lists = jnp.where(live, hub_list[0], -1).astype(bf16).T
    lists = jnp.pad(lists, ((0, 0), (0, 128 - blocks)), constant_values=-1)
    theirs = permute(features, SWAP_Y)
    their_lists = permute(lists, SWAP_Y)

    bias_hi = as_bf16(bias)
    bias_mid = as_bf16(bias - bias_hi)
    bias_lo = bias - bias_hi - bias_mid
    bias_rows = jnp.stack([bias_hi, bias_mid, bias_lo]).astype(bf16)
    bias_rows = jnp.pad(bias_rows, ((0, 13), (0, 0)))
    packed = jnp.concatenate([self_weight, neighbor_weight, cotangent, bias_rows], axis=0)

    col0 = jnp.concatenate([features, theirs, lists, their_lists], axis=0)
    code = (tile_target[0] * 2 + tile_source[0]).reshape(-1)
    table = jnp.concatenate([code, tile_count[0]])
    col0, table, ids, packed = lax.optimization_barrier((col0, table, ids, packed))
    other = permute(packed, SWAP_R)
    cols = [permute(col0, FROM_COL[k]) for k in range(1, 5)]
    oth0 = permute(col0, SWAP_C)
    cols = jnp.concatenate(cols, axis=0)
    far = permute(cols, FROM_COL[4])
    oth1 = permute(cols, SWAP_C)
    mats_near = densify(NEAR, ids, table, tile_values)
    mats_far = densify(FAR, ids, table, tile_values)
    oth2 = permute(far, SWAP_C)

    partial, hot_near, wts_near = forward(
        NEAR, True, ids, col0, cols, oth0, oth1, mats_near, hub_weight
    )
    partial, hot_far, wts_far = forward(FAR, False, ids, far, oth2, mats_far, hub_weight, partial)
    theirs = permute(partial, SWAP_R)
    output, grad, self_grad, parts, give_parts = middle(
        ids,
        partial,
        theirs,
        features,
        self_weight,
        neighbor_weight,
        cotangent,
        bias[None, :],
        other,
    )

    with_far = (grad, mats_far, hot_far, wts_far)
    with_near = (grad, mats_near, hot_near, wts_near)
    got_far = permute(backward(1, FAR, bf16, ids, *with_far), SWAP_C)
    got_near = permute(backward(1, NEAR, bf16, ids, *with_near), SWAP_C)
    got_parts = permute(give_parts, SWAP_C)
    sent = backward(0, FAR, bf16, ids, *with_far, got_far)
    far_sums = permute(sent, inverse(FROM_COL[4]))
    keep = backward(0, NEAR, f32, ids, *with_near, got_near)

    def added(*terms):
        while len(terms) > 1:
            terms = [a + b for a, b in zip(terms[::2], terms[1::2])]
        return terms[0]

    def over_columns(value, routes):
        return added(value, *(permute(value, p) for p in routes))

    parts = added(parts, got_parts)
    quarter = added(parts[0], permute(parts[1], SWAP_L))
    quarter = over_columns(quarter, SAME_X)
    far_sums, _ = lax.optimization_barrier((far_sums, quarter))

    piece = ((128, 512), bf16)
    near = kernel_call(near_kernel, 2, [piece] * 4)(ids, keep, far_sums)
    got = [permute(near[k - 1], inverse(FROM_COL[k])) for k in range(1, 5)]
    quarter = over_columns(quarter, SAME_Z)
    line = permute(quarter, SWAP_L)
    core = permute(jnp.stack([quarter, line]), SWAP_C)
    piece = ((128, 256), bf16)
    same, cross = kernel_call(mine_kernel, 5, [piece] * 2)(ids, keep, *got)
    over = permute(same, SWAP_R)
    down = permute(cross, FROM_DOWN)
    up = permute(cross, FROM_UP)
    grad_input = kernel_call(finish_kernel, 5, ((256, 128), bf16))(
        ids, same, over, down, up, self_grad
    )
    grad_self, grad_neighbor, grad_bias = kernel_call(
        functools.partial(weights_kernel, 1.0 / math.sqrt(256 * blocks)),
        3,
        [((128, 128), f32), ((128, 128), f32), ((1, 128), f32)],
        scratch=[pltpu.VMEM((256, 128), f32), pltpu.VMEM((4, PART - 64, 128), f32)],
    )(ids, quarter, line, core)
    return output, grad_input, grad_self, grad_neighbor, grad_bias[0]


def solution(mesh):
    in_specs = (
        P("blk", None),
        P("blk", "rep", None, None, None),
        P("blk", "rep", None),
        P("blk", "rep", None),
        P("blk", "rep"),
        P("blk", None, None),
        P("blk", None),
        P(None, None, "blk"),
        P(None, "rep"),
        P(None, "rep"),
        P("rep"),
        P("blk", "rep"),
    )
    out_specs = (P("blk", "rep"), P("blk", None), P(None, "rep"), P(None, "rep"), P("rep"))
    return jax.shard_map(layer, mesh=mesh, in_specs=in_specs, out_specs=out_specs, check_vma=False)
```

```python
import functools
import math

import jax
import jax.numpy as jnp
from jax import lax
from jax.experimental import pallas as pl
from jax.experimental.pallas import tpu as pltpu
from jax.sharding import PartitionSpec as P


AXES = ("blk", "rep")
COLS = 9
HEAD = 16
PART = 64 + 8
GROUP = 2 * (256 + HEAD)
MIB = 2**20


def route(source_of):
    pairs = []
    for block in range(64):
        for r in range(2):
            q, l, c = block // 4, (block // 2) % 2, block % 2
            q2, l2, c2, r2 = source_of(q, l, c, r)
            pairs.append(((((q2 % 16) * 2 + l2 % 2) * 2 + c2 % 2) * 2 + r2 % 2, block * 2 + r))
    return pairs


def inverse(pairs):
    return [(d, s) for s, d in pairs]


def y_step(step):
    def source(q, l, c, r):
        y = (2 * r + l + step(c)) % 4
        return (q, y % 2, c, y // 2)

    return route(source)


SWAP_Y = y_step(lambda c: 1 if c else -1)
FROM_DOWN = y_step(lambda c: -1)
FROM_UP = y_step(lambda c: 1)
SWAP_C = route(lambda q, l, c, r: (q, l, c + 1, r))
SWAP_L = route(lambda q, l, c, r: (q, l + 1, c, r))
SWAP_R = route(lambda q, l, c, r: (q, l, c, r + 1))
SAME_X, SAME_Z = (
    [route(lambda q, l, c, r, m=m: (q ^ m, l, c, r)) for m in masks]
    for masks in ((1, 3, 2), (4, 12, 8))
)
FROM_COL = [route(lambda q, l, c, r, k=k: (q + (k if r else -k), l, c, r)) for k in range(5)]


def permute(x, pairs):
    return lax.ppermute(x, AXES, pairs)


def as_bf16(x):
    return lax.reduce_precision(x, 8, 7)


def dot(a, b):
    return jnp.dot(a, b, preferred_element_type=jnp.float32)


def dot_nt(a, b):
    return lax.dot_general(a, b, (((1,), (1,)), ((), ())), preferred_element_type=jnp.float32)


def dot_tn(a, b):
    return lax.dot_general(a, b, (((0,), (0,)), ((), ())), preferred_element_type=jnp.float32)


def slot_source(ids_ref, cls, k, lr):
    block, r = ids_ref[0], ids_ref[1]
    q = lax.bitwise_and(block // 4 + jnp.where(r == 1, k, -k) + 16, 15)
    source = q * 4 + lax.bitwise_xor(lax.bitwise_and(block, 3), lr * 2 + cls)
    offset = lax.bitwise_and(block - source + 64, 63) - 32 * r
    return source, jnp.logical_and(offset >= 0, offset < 32)


def vmem():
    return pl.BlockSpec(memory_space=pltpu.VMEM)


def smem():
    return pl.BlockSpec(memory_space=pltpu.SMEM)


def kernel_call(body, n_in, outs, scratch=(), limit=8 * MIB):
    single = not isinstance(outs, list)
    shapes = [jax.ShapeDtypeStruct(*o) for o in ([outs] if single else outs)]

    def call(*args):
        return pl.pallas_call(
            body,
            in_specs=[smem()] + [vmem()] * n_in,
            out_specs=vmem() if single else [vmem()] * len(shapes),
            out_shape=shapes[0] if single else shapes,
            scratch_shapes=list(scratch),
            compiler_params=pltpu.CompilerParams(vmem_limit_bytes=limit),
        )(*args)

    return call


DEPTH = 12
QUAD = 4
NEAR, FAR = tuple(range(5)), tuple(range(5, COLS))


def densify_kernel(columns, ids_ref, table_ref, tiles_ref, out_ref, *scratch):
    acc_ref, buf_ref, sem_ref = scratch
    slots = 4 * len(columns)
    counts_at, width = tiles_ref.shape[1] * tiles_ref.shape[2], tiles_ref.shape[2]

    def place(slot):
        cls = slot // (2 * len(columns))
        k = columns[0] + lax.rem(slot // 2, len(columns))
        source, valid = slot_source(ids_ref, cls, k, lax.rem(slot, 2))
        offset = lax.bitwise_and(ids_ref[0] - source + 64, 63) - 32 * ids_ref[1]
        offset = jnp.where(valid, offset, 0)
        return offset, jnp.where(valid, table_ref[counts_at + offset], 0)

    def fetch(slot, act):
        offset, live = place(slot)
        at = lax.rem(slot, DEPTH)
        for i in range(0, width, QUAD):

            @pl.when(live > i)
            def _():
                act(
                    pltpu.make_async_copy(
                        tiles_ref.at[0, offset, pl.ds(i, QUAD)],
                        buf_ref.at[at, pl.ds(i, QUAD)],
                        sem_ref.at[at, i // QUAD],
                    )
                )

    def start(copy):
        copy.start()

    def wait(copy):
        copy.wait()

    for u in range(DEPTH):
        fetch(u, start)

    def body(slot, carry):
        at = lax.rem(slot, DEPTH)
        offset, live = place(slot)
        acc_ref[...] = jnp.zeros_like(acc_ref)
        fetch(slot, wait)

        def add(j, inner):
            code = table_ref[offset * width + j]
            acc_ref[code] += buf_ref[at, j].astype(jnp.float32)
            return inner

        lax.fori_loop(0, live, add, 0)

        @pl.when(slot + DEPTH < slots)
        def _():
            fetch(slot + DEPTH, start)

        for t in range(2):
            for s in range(2):
                out_ref[slot, t * 128 : (t + 1) * 128, s * 128 : (s + 1) * 128] = acc_ref[
                    t * 2 + s
                ].astype(jnp.bfloat16)
        return carry

    lax.fori_loop(0, slots, body, 0)


def densify(columns, ids, table, tile_values):
    return pl.pallas_call(
        functools.partial(densify_kernel, columns),
        in_specs=[smem()] * 2 + [pl.BlockSpec(memory_space=pltpu.HBM)],
        out_specs=vmem(),
        scratch_shapes=[
            pltpu.VMEM((4, 128, 128), jnp.float32),
            pltpu.VMEM((DEPTH,) + tile_values.shape[2:], jnp.bfloat16),
            pltpu.SemaphoreType.DMA((DEPTH, tile_values.shape[2] // QUAD)),
        ],
        out_shape=jax.ShapeDtypeStruct((4 * len(columns), 256, 256), jnp.bfloat16),
        compiler_params=pltpu.CompilerParams(vmem_limit_bytes=48 * MIB),
    )(ids, table, tile_values)


def join_kernel(ids_ref, *refs):
    for i, ref in enumerate(refs[:-1]):
        refs[-1][i * GROUP : (i + 1) * GROUP, :] = ref[...]


def forward_kernel(columns, first, ids_ref, *refs):
    groups, (mats_ref, hub_ref), refs = refs[: 4 if first else 2], refs[4 if first else 2 :][:2], refs[6 if first else 4 :]
    before_ref, (out_ref, hot_ref, wts_ref, pick_ref) = (None, refs) if first else (refs[0], refs[1:])
    lane = lax.broadcasted_iota(jnp.int32, (2 * HEAD, 128), 1)
    column = lax.broadcasted_iota(jnp.int32, (2 * HEAD, 256), 1)
    total = None if first else before_ref[...]
    for cls in range(2):
        for i, k in enumerate(columns):
            if first:
                ref, base = groups[cls * 2 + min(k, 1)], max(k - 1, 0) * GROUP
            else:
                ref, base = groups[cls], i * GROUP
            head = ref[base + 512 : base + GROUP, :].astype(jnp.float32)
            mine = jnp.sum(jnp.where(lane == ids_ref[0], head, 0.0), axis=1, keepdims=True)
            hot = (mine.astype(jnp.int32) == column).astype(jnp.float32).astype(jnp.bfloat16)
            for lr in range(2):
                slot = (cls * len(columns) + i) * 2 + lr
                source, valid = slot_source(ids_ref, cls, k, lr)
                at = slice(slot * HEAD, (slot + 1) * HEAD)
                one = hot[lr * HEAD : (lr + 1) * HEAD, :]
                block = ref[base + lr * 256 : base + (lr + 1) * 256, :]
                both = dot(jnp.concatenate([mats_ref[slot], one], axis=0), block)
                total = both[:256] if total is None else total + both[:256]
                hot_ref[at, :] = one
                pick_ref[at, :] = both[256:].astype(jnp.bfloat16)
                weights = hub_ref[source]
                wts_ref[at, :] = jnp.where(valid, weights, jnp.zeros_like(weights))
    out_ref[...] = (total + dot_tn(wts_ref[...], pick_ref[...])).astype(out_ref.dtype)


def forward(columns, first, *args):
    rows = 4 * len(columns) * HEAD
    return kernel_call(
        functools.partial(forward_kernel, columns, first),
        len(args) - 1,
        [
            ((256, 128), jnp.float32 if first else jnp.bfloat16),
            ((rows, 256), jnp.bfloat16),
            ((rows, 256), jnp.bfloat16),
        ],
        scratch=[pltpu.VMEM((rows, 128), jnp.bfloat16)],
        limit=20 * MIB,
    )(*args)


def middle_kernel(
    ids_ref, mine_ref, theirs_ref, feat_ref, sw_ref, nw_ref, ct_ref, bias_ref, other_ref, *outs
):
    out_ref, grad_ref, self_ref, keep_ref, give_ref, sums_ref = outs
    feats = feat_ref[...]
    agg = mine_ref[...].astype(jnp.float32) + theirs_ref[...].astype(jnp.float32)
    agg = agg.astype(jnp.bfloat16)

    def half(sw, nw, ct, bias):
        pre = dot(feats, sw) + dot(agg, nw) + bias
        gate = jax.nn.sigmoid(pre)
        act = ct.astype(jnp.float32) * gate * (1.0 + pre * (1.0 - gate))
        return pre * gate, act.astype(jnp.bfloat16)

    sw, nw = sw_ref[...], nw_ref[...]
    sw2, nw2 = other_ref[0:128, :], other_ref[128:256, :]
    extra = other_ref[512:528, :].astype(jnp.float32)
    bias2 = extra[0:1] + extra[1:2] + extra[2:3]
    value, act = half(sw, nw, ct_ref[...], bias_ref[...])
    _, act2 = half(sw2, nw2, other_ref[256:512, :], bias2)
    out_ref[...] = value.astype(jnp.bfloat16)
    grad_ref[...] = (dot_nt(nw, act) + dot_nt(nw2, act2)).astype(jnp.bfloat16)
    self_ref[...] = dot_nt(sw, act) + dot_nt(sw2, act2)
    sums_ref[0:128, :] = dot_tn(act, feats)
    sums_ref[128:256, :] = dot_tn(act, agg)
    bias_sum = jnp.sum(act.astype(jnp.float32), axis=0, keepdims=True)
    low = lax.bitwise_and(ids_ref[0], 3)
    for lr in range(2):
        for cls, ref in enumerate((keep_ref, give_ref)):
            quarter = lax.bitwise_xor(low, 2 * lr + cls)
            ref[lr, 0:64, :] = sums_ref[pl.ds(pl.multiple_of(quarter * 64, 64), 64), :]
            ref[lr, 64:PART, :] = jnp.broadcast_to(bias_sum, (PART - 64, 128))


def middle(*args):
    return kernel_call(
        middle_kernel,
        8,
        [
            ((256, 128), jnp.bfloat16),
            ((128, 256), jnp.bfloat16),
            ((128, 256), jnp.float32),
            ((2, PART, 128), jnp.float32),
            ((2, PART, 128), jnp.float32),
        ],
        scratch=[pltpu.VMEM((256, 128), jnp.float32)],
    )(*args)


def backward_kernel(cls, columns, add, ids_ref, grad_ref, mats_ref, hot_ref, wts_ref, *refs):
    out_ref = refs[-1]
    grad = grad_ref[...]
    count = 2 * len(columns) * HEAD
    backs = dot_nt(wts_ref[cls * count : (cls + 1) * count, :], grad).astype(jnp.bfloat16)
    for i in range(len(columns)):
        for lr in range(2):
            slot = (cls * len(columns) + i) * 2 + lr
            at = slice(slot * HEAD, (slot + 1) * HEAD)
            lanes = slice(lr * 256, (lr + 1) * 256)
            back = backs[(2 * i + lr) * HEAD : (2 * i + lr + 1) * HEAD]
            part = dot(grad, mats_ref[slot]) + dot_tn(back, hot_ref[at, :])
            if add:
                part += refs[0][i, :, lanes].astype(jnp.float32)
            out_ref[i, :, lanes] = part.astype(out_ref.dtype)


def backward(cls, columns, dtype, *args):
    body = functools.partial(backward_kernel, cls, columns, len(args) > 5)
    return kernel_call(body, len(args) - 1, ((len(columns), 128, 512), dtype), limit=20 * MIB)(
        *args
    )


def near_kernel(ids_ref, keep_ref, far_ref, *outs):
    for i, out in enumerate(outs):
        out[...] = (keep_ref[i + 1] + far_ref[i].astype(jnp.float32)).astype(jnp.bfloat16)


def mine_kernel(ids_ref, keep_ref, *refs):
    got, (same_ref, cross_ref) = refs[:4], refs[4:]
    total = keep_ref[0]
    for ref in got:
        total += ref[...].astype(jnp.float32)
    same_ref[...] = total[:, :256].astype(jnp.bfloat16)
    cross_ref[...] = total[:, 256:].astype(jnp.bfloat16)


def finish_kernel(scale, ids_ref, *refs):
    f32 = jnp.float32
    same_ref, rep_ref, down_ref, up_ref, add_ref = refs[:5]
    parts, (grad_ref, self_ref, neighbor_ref, bias_ref, sums_ref, bias_sums_ref) = refs[5:9], refs[9:]
    total = (same_ref[...].astype(f32) + rep_ref[...].astype(f32)) + (
        down_ref[...].astype(f32) + up_ref[...].astype(f32)
    )
    grad_ref[...] = (total + add_ref[...]).T.astype(jnp.bfloat16)
    low = lax.bitwise_and(ids_ref[0], 3)
    for lr in range(2):
        for cls in range(2):
            part = parts[2 * cls + lr]
            quarter = lax.bitwise_xor(low, 2 * lr + cls)
            sums_ref[pl.ds(pl.multiple_of(quarter * 64, 64), 64), :] = part[0:64, :]
            bias_sums_ref[quarter] = part[64:PART, :]
    self_ref[...] = sums_ref[0:128, :].T * scale
    neighbor_ref[...] = sums_ref[128:256, :].T * scale
    bias_ref[...] = bias_sums_ref[0][0:1] * scale


def layer(
    features,
    tile_values,
    tile_target,
    tile_source,
    tile_count,
    hub_list,
    hub_count,
    hub_weight,
    self_weight,
    neighbor_weight,
    bias,
    cotangent,
):
    f32, bf16 = jnp.float32, jnp.bfloat16
    blocks = lax.axis_size("blk")
    ids = jnp.stack([lax.axis_index("blk"), lax.axis_index("rep")]).astype(jnp.int32)

    live = jnp.arange(HEAD, dtype=jnp.int32)[None, :] < hub_count[0][:, None]
    lists = jnp.where(live, hub_list[0], -1).astype(bf16).T
    lists = jnp.pad(lists, ((0, 0), (0, 128 - blocks)), constant_values=-1)
    theirs = permute(features, SWAP_Y)
    their_lists = permute(lists, SWAP_Y)

    bias_hi = as_bf16(bias)
    bias_mid = as_bf16(bias - bias_hi)
    bias_lo = bias - bias_hi - bias_mid
    bias_rows = jnp.stack([bias_hi, bias_mid, bias_lo]).astype(bf16)
    bias_rows = jnp.pad(bias_rows, ((0, 13), (0, 0)))
    packed = jnp.concatenate([self_weight, neighbor_weight, cotangent, bias_rows], axis=0)

    col0 = jnp.concatenate([features, theirs, lists, their_lists], axis=0)
    code = (tile_target[0] * 2 + tile_source[0]).reshape(-1)
    table = jnp.concatenate([code, tile_count[0]])
    col0, table, ids, packed = lax.optimization_barrier((col0, table, ids, packed))
    other = permute(packed, SWAP_R)
    cols = [permute(col0, FROM_COL[k]) for k in range(1, 5)]
    oth0 = permute(col0, SWAP_C)
    cols = kernel_call(join_kernel, 4, ((4 * GROUP, 128), bf16))(ids, *cols)
    far = permute(cols, FROM_COL[4])
    oth1 = permute(cols, SWAP_C)
    mats_near = densify(NEAR, ids, table, tile_values)
    mats_far = densify(FAR, ids, table, tile_values)
    oth2 = permute(far, SWAP_C)

    partial, hot_near, wts_near = forward(
        NEAR, True, ids, col0, cols, oth0, oth1, mats_near, hub_weight
    )
    partial, hot_far, wts_far = forward(FAR, False, ids, far, oth2, mats_far, hub_weight, partial)
    theirs = permute(partial, SWAP_R)
    output, grad, self_grad, parts, give_parts = middle(
        ids,
        partial,
        theirs,
        features,
        self_weight,
        neighbor_weight,
        cotangent,
        bias[None, :],
        other,
    )

    with_far = (grad, mats_far, hot_far, wts_far)
    with_near = (grad, mats_near, hot_near, wts_near)
    got_far = permute(backward(1, FAR, bf16, ids, *with_far), SWAP_C)
    got_near = permute(backward(1, NEAR, bf16, ids, *with_near), SWAP_C)
    got_parts = permute(give_parts, SWAP_C)
    sent = backward(0, FAR, bf16, ids, *with_far, got_far)
    far_sums = permute(sent, inverse(FROM_COL[4]))
    keep = backward(0, NEAR, f32, ids, *with_near, got_near)

    def added(*terms):
        while len(terms) > 1:
            terms = [a + b for a, b in zip(terms[::2], terms[1::2])]
        return terms[0]

    def over_columns(value, routes):
        return added(value, *(permute(value, p) for p in routes))

    parts = added(parts, got_parts)
    quarter = added(parts[0], permute(parts[1], SWAP_L))
    quarter = over_columns(quarter, SAME_X)
    far_sums, _ = lax.optimization_barrier((far_sums, quarter))

    piece = ((128, 512), bf16)
    near = kernel_call(near_kernel, 2, [piece] * 4)(ids, keep, far_sums)
    got = [permute(near[k - 1], inverse(FROM_COL[k])) for k in range(1, 5)]
    quarter = over_columns(quarter, SAME_Z)
    line = permute(quarter, SWAP_L)
    core0, core1 = permute(quarter, SWAP_C), permute(line, SWAP_C)
    piece = ((128, 256), bf16)
    same, cross = kernel_call(mine_kernel, 5, [piece] * 2)(ids, keep, *got)
    over = permute(same, SWAP_R)
    down = permute(cross, FROM_DOWN)
    up = permute(cross, FROM_UP)
    grad_input, grad_self, grad_neighbor, grad_bias = kernel_call(
        functools.partial(finish_kernel, 1.0 / math.sqrt(256 * blocks)),
        9,
        [((256, 128), bf16), ((128, 128), f32), ((128, 128), f32), ((1, 128), f32)],
        scratch=[pltpu.VMEM((256, 128), f32), pltpu.VMEM((4, PART - 64, 128), f32)],
    )(ids, same, over, down, up, self_grad, quarter, line, core0, core1)
    return output, grad_input, grad_self, grad_neighbor, grad_bias[0]


def solution(mesh):
    in_specs = (
        P("blk", None),
        P("blk", "rep", None, None, None),
        P("blk", "rep", None),
        P("blk", "rep", None),
        P("blk", "rep"),
        P("blk", None, None),
        P("blk", None),
        P(None, None, "blk"),
        P(None, "rep"),
        P(None, "rep"),
        P("rep"),
        P("blk", "rep"),
    )
    out_specs = (P("blk", "rep"), P("blk", None), P(None, "rep"), P(None, "rep"), P("rep"))
    return jax.shard_map(layer, mesh=mesh, in_specs=in_specs, out_specs=out_specs, check_vma=False)
```

```python
import functools
import math

import jax
import jax.numpy as jnp
from jax import lax
from jax.experimental import pallas as pl
from jax.experimental.pallas import tpu as pltpu
from jax.sharding import PartitionSpec as P


AXES = ("blk", "rep")
COLS = 9
HEAD = 16
PART = 64 + 8
GROUP = 2 * (256 + HEAD)
MIB = 2**20


def route(source_of):
    pairs = []
    for block in range(64):
        for r in range(2):
            q, l, c = block // 4, (block // 2) % 2, block % 2
            q2, l2, c2, r2 = source_of(q, l, c, r)
            pairs.append(((((q2 % 16) * 2 + l2 % 2) * 2 + c2 % 2) * 2 + r2 % 2, block * 2 + r))
    return pairs


def inverse(pairs):
    return [(d, s) for s, d in pairs]


def y_step(step):
    def source(q, l, c, r):
        y = (2 * r + l + step(c)) % 4
        return (q, y % 2, c, y // 2)

    return route(source)


SWAP_Y = y_step(lambda c: 1 if c else -1)
FROM_DOWN = y_step(lambda c: -1)
FROM_UP = y_step(lambda c: 1)
SWAP_C = route(lambda q, l, c, r: (q, l, c + 1, r))
SWAP_L = route(lambda q, l, c, r: (q, l + 1, c, r))
SWAP_R = route(lambda q, l, c, r: (q, l, c, r + 1))
SAME_X, SAME_Z = (
    [route(lambda q, l, c, r, m=m: (q ^ m, l, c, r)) for m in masks]
    for masks in ((1, 3, 2), (4, 12, 8))
)
FROM_COL = [route(lambda q, l, c, r, k=k: (q + (k if r else -k), l, c, r)) for k in range(5)]


def permute(x, pairs):
    return lax.ppermute(x, AXES, pairs)


def as_bf16(x):
    return lax.reduce_precision(x, 8, 7)


def dot(a, b):
    return jnp.dot(a, b, preferred_element_type=jnp.float32)


def dot_nt(a, b):
    return lax.dot_general(a, b, (((1,), (1,)), ((), ())), preferred_element_type=jnp.float32)


def dot_tn(a, b):
    return lax.dot_general(a, b, (((0,), (0,)), ((), ())), preferred_element_type=jnp.float32)


def slot_source(ids_ref, cls, k, lr):
    block, r = ids_ref[0], ids_ref[1]
    q = lax.bitwise_and(block // 4 + jnp.where(r == 1, k, -k) + 16, 15)
    source = q * 4 + lax.bitwise_xor(lax.bitwise_and(block, 3), lr * 2 + cls)
    offset = lax.bitwise_and(block - source + 64, 63) - 32 * r
    return source, jnp.logical_and(offset >= 0, offset < 32)


def vmem():
    return pl.BlockSpec(memory_space=pltpu.VMEM)


def smem():
    return pl.BlockSpec(memory_space=pltpu.SMEM)


def kernel_call(body, n_in, outs, scratch=(), limit=8 * MIB):
    single = not isinstance(outs, list)
    shapes = [jax.ShapeDtypeStruct(*o) for o in ([outs] if single else outs)]

    def call(*args):
        return pl.pallas_call(
            body,
            in_specs=[smem()] + [vmem()] * n_in,
            out_specs=vmem() if single else [vmem()] * len(shapes),
            out_shape=shapes[0] if single else shapes,
            scratch_shapes=list(scratch),
            compiler_params=pltpu.CompilerParams(vmem_limit_bytes=limit),
        )(*args)

    return call


DEPTH = 12
QUAD = 4
NEAR, FAR = tuple(range(5)), tuple(range(5, COLS))


def densify_kernel(columns, ids_ref, table_ref, tiles_ref, out_ref, *scratch):
    acc_ref, buf_ref, sem_ref = scratch
    slots = 4 * len(columns)
    counts_at, width = tiles_ref.shape[1] * tiles_ref.shape[2], tiles_ref.shape[2]

    def place(slot):
        cls = slot // (2 * len(columns))
        k = columns[0] + lax.rem(slot // 2, len(columns))
        source, valid = slot_source(ids_ref, cls, k, lax.rem(slot, 2))
        offset = lax.bitwise_and(ids_ref[0] - source + 64, 63) - 32 * ids_ref[1]
        offset = jnp.where(valid, offset, 0)
        return offset, jnp.where(valid, table_ref[counts_at + offset], 0)

    def fetch(slot, act):
        offset, live = place(slot)
        at = lax.rem(slot, DEPTH)
        for i in range(0, width, QUAD):

            @pl.when(live > i)
            def _():
                act(
                    pltpu.make_async_copy(
                        tiles_ref.at[0, offset, pl.ds(i, QUAD)],
                        buf_ref.at[at, pl.ds(i, QUAD)],
                        sem_ref.at[at, i // QUAD],
                    )
                )

    def start(copy):
        copy.start()

    def wait(copy):
        copy.wait()

    for u in range(DEPTH):
        fetch(u, start)

    def body(slot, carry):
        at = lax.rem(slot, DEPTH)
        offset, live = place(slot)
        acc_ref[...] = jnp.zeros_like(acc_ref)
        fetch(slot, wait)

        def add(j, inner):
            code = table_ref[offset * width + j]
            acc_ref[code] += buf_ref[at, j].astype(jnp.float32)
            return inner

        lax.fori_loop(0, live, add, 0)

        @pl.when(slot + DEPTH < slots)
        def _():
            fetch(slot + DEPTH, start)

        for t in range(2):
            for s in range(2):
                out_ref[slot, t * 128 : (t + 1) * 128, s * 128 : (s + 1) * 128] = acc_ref[
                    t * 2 + s
                ].astype(jnp.bfloat16)
        return carry

    lax.fori_loop(0, slots, body, 0)


def densify(columns, ids, table, tile_values):
    return pl.pallas_call(
        functools.partial(densify_kernel, columns),
        in_specs=[smem()] * 2 + [pl.BlockSpec(memory_space=pltpu.HBM)],
        out_specs=vmem(),
        scratch_shapes=[
            pltpu.VMEM((4, 128, 128), jnp.float32),
            pltpu.VMEM((DEPTH,) + tile_values.shape[2:], jnp.bfloat16),
            pltpu.SemaphoreType.DMA((DEPTH, tile_values.shape[2] // QUAD)),
        ],
        out_shape=jax.ShapeDtypeStruct((4 * len(columns), 256, 256), jnp.bfloat16),
        compiler_params=pltpu.CompilerParams(vmem_limit_bytes=48 * MIB),
    )(ids, table, tile_values)


def join_kernel(ids_ref, *refs):
    for i, ref in enumerate(refs[:4]):
        for out in refs[4:] if i < 3 else refs[4:5]:
            out[i * GROUP : (i + 1) * GROUP, :] = ref[...]


def forward_kernel(columns, first, ids_ref, *refs):
    groups, (mats_ref, hub_ref), refs = refs[:4], refs[4:6], refs[6:]
    before_ref, (out_ref, hot_ref, wts_ref, pick_ref) = (None, refs) if first else (refs[0], refs[1:])
    lane = lax.broadcasted_iota(jnp.int32, (2 * HEAD, 128), 1)
    column = lax.broadcasted_iota(jnp.int32, (2 * HEAD, 256), 1)
    total = None if first else before_ref[...]
    for cls in range(2):
        for i, k in enumerate(columns):
            if first:
                ref, base = groups[cls * 2 + min(k, 1)], max(k - 1, 0) * GROUP
            else:
                ref, base = groups[cls * 2 + i // 3], i % 3 * GROUP
            head = ref[base + 512 : base + GROUP, :].astype(jnp.float32)
            mine = jnp.sum(jnp.where(lane == ids_ref[0], head, 0.0), axis=1, keepdims=True)
            hot = (mine.astype(jnp.int32) == column).astype(jnp.float32).astype(jnp.bfloat16)
            for lr in range(2):
                slot = (cls * len(columns) + i) * 2 + lr
                source, valid = slot_source(ids_ref, cls, k, lr)
                at = slice(slot * HEAD, (slot + 1) * HEAD)
                one = hot[lr * HEAD : (lr + 1) * HEAD, :]
                block = ref[base + lr * 256 : base + (lr + 1) * 256, :]
                both = dot(jnp.concatenate([mats_ref[slot], one], axis=0), block)
                total = both[:256] if total is None else total + both[:256]
                hot_ref[at, :] = one
                pick_ref[at, :] = both[256:].astype(jnp.bfloat16)
                weights = hub_ref[source]
                wts_ref[at, :] = jnp.where(valid, weights, jnp.zeros_like(weights))
    out_ref[...] = (total + dot_tn(wts_ref[...], pick_ref[...])).astype(out_ref.dtype)


def forward(columns, first, *args):
    rows = 4 * len(columns) * HEAD
    return kernel_call(
        functools.partial(forward_kernel, columns, first),
        len(args) - 1,
        [
            ((256, 128), jnp.float32 if first else jnp.bfloat16),
            ((rows, 256), jnp.bfloat16),
            ((rows, 256), jnp.bfloat16),
        ],
        scratch=[pltpu.VMEM((rows, 128), jnp.bfloat16)],
        limit=20 * MIB,
    )(*args)


def middle_kernel(
    ids_ref, mine_ref, theirs_ref, feat_ref, sw_ref, nw_ref, ct_ref, bias_ref, other_ref, *outs
):
    out_ref, grad_ref, self_ref, keep_ref, give_ref, sums_ref = outs
    feats = feat_ref[...]
    agg = mine_ref[...].astype(jnp.float32) + theirs_ref[...].astype(jnp.float32)
    agg = agg.astype(jnp.bfloat16)

    def half(sw, nw, ct, bias):
        pre = dot(feats, sw) + dot(agg, nw) + bias
        gate = jax.nn.sigmoid(pre)
        act = ct.astype(jnp.float32) * gate * (1.0 + pre * (1.0 - gate))
        return pre * gate, act.astype(jnp.bfloat16)

    sw, nw = sw_ref[...], nw_ref[...]
    sw2, nw2 = other_ref[0:128, :], other_ref[128:256, :]
    extra = other_ref[512:528, :].astype(jnp.float32)
    bias2 = extra[0:1] + extra[1:2] + extra[2:3]
    value, act = half(sw, nw, ct_ref[...], bias_ref[...])
    _, act2 = half(sw2, nw2, other_ref[256:512, :], bias2)
    out_ref[...] = value.astype(jnp.bfloat16)
    grad_ref[...] = (dot_nt(nw, act) + dot_nt(nw2, act2)).astype(jnp.bfloat16)
    self_ref[...] = dot_nt(sw, act) + dot_nt(sw2, act2)
    sums_ref[0:128, :] = dot_tn(act, feats)
    sums_ref[128:256, :] = dot_tn(act, agg)
    bias_sum = jnp.sum(act.astype(jnp.float32), axis=0, keepdims=True)
    low = lax.bitwise_and(ids_ref[0], 3)
    for lr in range(2):
        for cls, ref in enumerate((keep_ref, give_ref)):
            quarter = lax.bitwise_xor(low, 2 * lr + cls)
            ref[lr, 0:64, :] = sums_ref[pl.ds(pl.multiple_of(quarter * 64, 64), 64), :]
            ref[lr, 64:PART, :] = jnp.broadcast_to(bias_sum, (PART - 64, 128))


def middle(*args):
    return kernel_call(
        middle_kernel,
        8,
        [
            ((256, 128), jnp.bfloat16),
            ((128, 256), jnp.bfloat16),
            ((128, 256), jnp.float32),
            ((2, PART, 128), jnp.float32),
            ((2, PART, 128), jnp.float32),
        ],
        scratch=[pltpu.VMEM((256, 128), jnp.float32)],
    )(*args)


def backward_kernel(cls, columns, add, ids_ref, grad_ref, mats_ref, hot_ref, wts_ref, *refs):
    out_ref = refs[-1]
    grad = grad_ref[...]
    count = 2 * len(columns) * HEAD
    backs = dot_nt(wts_ref[cls * count : (cls + 1) * count, :], grad).astype(jnp.bfloat16)
    for i in range(len(columns)):
        for lr in range(2):
            slot = (cls * len(columns) + i) * 2 + lr
            at = slice(slot * HEAD, (slot + 1) * HEAD)
            lanes = slice(lr * 256, (lr + 1) * 256)
            back = backs[(2 * i + lr) * HEAD : (2 * i + lr + 1) * HEAD]
            part = dot(grad, mats_ref[slot]) + dot_tn(back, hot_ref[at, :])
            if add:
                part += refs[0][i, :, lanes].astype(jnp.float32)
            out_ref[i, :, lanes] = part.astype(out_ref.dtype)


def backward(cls, columns, dtype, *args):
    body = functools.partial(backward_kernel, cls, columns, len(args) > 5)
    return kernel_call(body, len(args) - 1, ((len(columns), 128, 512), dtype), limit=20 * MIB)(
        *args
    )


def near_kernel(ids_ref, keep_ref, far_ref, *outs):
    for i, out in enumerate(outs):
        out[...] = (keep_ref[i + 1] + far_ref[i].astype(jnp.float32)).astype(jnp.bfloat16)


def mine_kernel(ids_ref, keep_ref, *refs):
    got, (same_ref, cross_ref) = refs[:4], refs[4:]
    total = keep_ref[0]
    for ref in got:
        total += ref[...].astype(jnp.float32)
    same_ref[...] = total[:, :256].astype(jnp.bfloat16)
    cross_ref[...] = total[:, 256:].astype(jnp.bfloat16)


def finish_kernel(scale, ids_ref, *refs):
    f32 = jnp.float32
    same_ref, rep_ref, down_ref, up_ref, add_ref = refs[:5]
    parts, (grad_ref, self_ref, neighbor_ref, bias_ref, sums_ref, bias_sums_ref) = refs[5:9], refs[9:]
    total = (same_ref[...].astype(f32) + rep_ref[...].astype(f32)) + (
        down_ref[...].astype(f32) + up_ref[...].astype(f32)
    )
    grad_ref[...] = (total + add_ref[...]).T.astype(jnp.bfloat16)
    low = lax.bitwise_and(ids_ref[0], 3)
    for lr in range(2):
        for cls in range(2):
            part = parts[2 * cls + lr]
            quarter = lax.bitwise_xor(low, 2 * lr + cls)
            sums_ref[pl.ds(pl.multiple_of(quarter * 64, 64), 64), :] = part[0:64, :]
            bias_sums_ref[quarter] = part[64:PART, :]
    self_ref[...] = sums_ref[0:128, :].T * scale
    neighbor_ref[...] = sums_ref[128:256, :].T * scale
    bias_ref[...] = bias_sums_ref[0][0:1] * scale


def layer(
    features,
    tile_values,
    tile_target,
    tile_source,
    tile_count,
    hub_list,
    hub_count,
    hub_weight,
    self_weight,
    neighbor_weight,
    bias,
    cotangent,
):
    f32, bf16 = jnp.float32, jnp.bfloat16
    blocks = lax.axis_size("blk")
    ids = jnp.stack([lax.axis_index("blk"), lax.axis_index("rep")]).astype(jnp.int32)

    live = jnp.arange(HEAD, dtype=jnp.int32)[None, :] < hub_count[0][:, None]
    lists = jnp.where(live, hub_list[0], -1).astype(bf16).T
    lists = jnp.pad(lists, ((0, 0), (0, 128 - blocks)), constant_values=-1)
    theirs = permute(features, SWAP_Y)
    their_lists = permute(lists, SWAP_Y)

    bias_hi = as_bf16(bias)
    bias_mid = as_bf16(bias - bias_hi)
    bias_lo = bias - bias_hi - bias_mid
    bias_rows = jnp.stack([bias_hi, bias_mid, bias_lo]).astype(bf16)
    bias_rows = jnp.pad(bias_rows, ((0, 13), (0, 0)))
    packed = jnp.concatenate([self_weight, neighbor_weight, cotangent, bias_rows], axis=0)

    col0 = jnp.concatenate([features, theirs, lists, their_lists], axis=0)
    code = (tile_target[0] * 2 + tile_source[0]).reshape(-1)
    table = jnp.concatenate([code, tile_count[0]])
    col0, table, ids, packed = lax.optimization_barrier((col0, table, ids, packed))
    other = permute(packed, SWAP_R)
    cols = [permute(col0, FROM_COL[k]) for k in range(1, 5)]
    oth0 = permute(col0, SWAP_C)
    turn = permute(col0, inverse(FROM_COL[4]))
    cols, sent = kernel_call(
        join_kernel, 4, [((4 * GROUP, 128), bf16), ((3 * GROUP, 128), bf16)]
    )(ids, *cols)
    far = permute(sent, FROM_COL[4])
    last = permute(turn, inverse(FROM_COL[4]))
    oth1 = permute(cols, SWAP_C)
    mats_near = densify(NEAR, ids, table, tile_values)
    mats_far = densify(FAR, ids, table, tile_values)
    oth2 = permute(far, SWAP_C)
    oth3 = permute(last, SWAP_C)

    partial, hot_near, wts_near = forward(
        NEAR, True, ids, col0, cols, oth0, oth1, mats_near, hub_weight
    )
    partial, hot_far, wts_far = forward(
        FAR, False, ids, far, last, oth2, oth3, mats_far, hub_weight, partial
    )
    theirs = permute(partial, SWAP_R)
    output, grad, self_grad, parts, give_parts = middle(
        ids,
        partial,
        theirs,
        features,
        self_weight,
        neighbor_weight,
        cotangent,
        bias[None, :],
        other,
    )

    with_far = (grad, mats_far, hot_far, wts_far)
    with_near = (grad, mats_near, hot_near, wts_near)
    got_far = permute(backward(1, FAR, bf16, ids, *with_far), SWAP_C)
    got_near = permute(backward(1, NEAR, bf16, ids, *with_near), SWAP_C)
    got_parts = permute(give_parts, SWAP_C)
    sent = backward(0, FAR, bf16, ids, *with_far, got_far)
    far_sums = permute(sent, inverse(FROM_COL[4]))
    keep = backward(0, NEAR, f32, ids, *with_near, got_near)

    def added(*terms):
        while len(terms) > 1:
            terms = [a + b for a, b in zip(terms[::2], terms[1::2])]
        return terms[0]

    def over_columns(value, routes):
        return added(value, *(permute(value, p) for p in routes))

    parts = added(parts, got_parts)
    quarter = added(parts[0], permute(parts[1], SWAP_L))
    quarter = over_columns(quarter, SAME_X)
    far_sums, _ = lax.optimization_barrier((far_sums, quarter))

    piece = ((128, 512), bf16)
    near = kernel_call(near_kernel, 2, [piece] * 4)(ids, keep, far_sums)
    got = [permute(near[k - 1], inverse(FROM_COL[k])) for k in range(1, 5)]
    quarter = over_columns(quarter, SAME_Z)
    line = permute(quarter, SWAP_L)
    core0, core1 = permute(quarter, SWAP_C), permute(line, SWAP_C)
    piece = ((128, 256), bf16)
    same, cross = kernel_call(mine_kernel, 5, [piece] * 2)(ids, keep, *got)
    over = permute(same, SWAP_R)
    down = permute(cross, FROM_DOWN)
    up = permute(cross, FROM_UP)
    grad_input, grad_self, grad_neighbor, grad_bias = kernel_call(
        functools.partial(finish_kernel, 1.0 / math.sqrt(256 * blocks)),
        9,
        [((256, 128), bf16), ((128, 128), f32), ((128, 128), f32), ((1, 128), f32)],
        scratch=[pltpu.VMEM((256, 128), f32), pltpu.VMEM((4, PART - 64, 128), f32)],
    )(ids, same, over, down, up, self_grad, quarter, line, core0, core1)
    return output, grad_input, grad_self, grad_neighbor, grad_bias[0]


def solution(mesh):
    in_specs = (
        P("blk", None),
        P("blk", "rep", None, None, None),
        P("blk", "rep", None),
        P("blk", "rep", None),
        P("blk", "rep"),
        P("blk", None, None),
        P("blk", None),
        P(None, None, "blk"),
        P(None, "rep"),
        P(None, "rep"),
        P("rep"),
        P("blk", "rep"),
    )
    out_specs = (P("blk", "rep"), P("blk", None), P(None, "rep"), P(None, "rep"), P("rep"))
    return jax.shard_map(layer, mesh=mesh, in_specs=in_specs, out_specs=out_specs, check_vma=False)
```

```python
import functools
import math

import jax
import jax.numpy as jnp
from jax import lax
from jax.experimental import pallas as pl
from jax.experimental.pallas import tpu as pltpu
from jax.sharding import PartitionSpec as P


AXES = ("blk", "rep")
COLS = 9
HEAD = 16
PART = 64 + 8
GROUP = 2 * (256 + HEAD)
MIB = 2**20


def route(source_of):
    pairs = []
    for block in range(64):
        for r in range(2):
            q, l, c = block // 4, (block // 2) % 2, block % 2
            q2, l2, c2, r2 = source_of(q, l, c, r)
            pairs.append(((((q2 % 16) * 2 + l2 % 2) * 2 + c2 % 2) * 2 + r2 % 2, block * 2 + r))
    return pairs


def inverse(pairs):
    return [(d, s) for s, d in pairs]


def y_step(step):
    def source(q, l, c, r):
        y = (2 * r + l + step(c)) % 4
        return (q, y % 2, c, y // 2)

    return route(source)


SWAP_Y = y_step(lambda c: 1 if c else -1)
FROM_DOWN = y_step(lambda c: -1)
FROM_UP = y_step(lambda c: 1)
SWAP_C = route(lambda q, l, c, r: (q, l, c + 1, r))
SWAP_L = route(lambda q, l, c, r: (q, l + 1, c, r))
SWAP_R = route(lambda q, l, c, r: (q, l, c, r + 1))
SAME_X, SAME_Z = (
    [route(lambda q, l, c, r, m=m: (q ^ m, l, c, r)) for m in masks]
    for masks in ((1, 3, 2), (4, 12, 8))
)
FROM_COL = [route(lambda q, l, c, r, k=k: (q + (k if r else -k), l, c, r)) for k in range(5)]


def permute(x, pairs):
    return lax.ppermute(x, AXES, pairs)


def as_bf16(x):
    return lax.reduce_precision(x, 8, 7)


def dot(a, b):
    return jnp.dot(a, b, preferred_element_type=jnp.float32)


def dot_nt(a, b):
    return lax.dot_general(a, b, (((1,), (1,)), ((), ())), preferred_element_type=jnp.float32)


def dot_tn(a, b):
    return lax.dot_general(a, b, (((0,), (0,)), ((), ())), preferred_element_type=jnp.float32)


def slot_source(ids_ref, cls, k, lr):
    block, r = ids_ref[0], ids_ref[1]
    q = lax.bitwise_and(block // 4 + jnp.where(r == 1, k, -k) + 16, 15)
    source = q * 4 + lax.bitwise_xor(lax.bitwise_and(block, 3), lr * 2 + cls)
    offset = lax.bitwise_and(block - source + 64, 63) - 32 * r
    return source, jnp.logical_and(offset >= 0, offset < 32)


def vmem():
    return pl.BlockSpec(memory_space=pltpu.VMEM)


def smem():
    return pl.BlockSpec(memory_space=pltpu.SMEM)


def kernel_call(body, n_in, outs, scratch=(), limit=8 * MIB):
    single = not isinstance(outs, list)
    shapes = [jax.ShapeDtypeStruct(*o) for o in ([outs] if single else outs)]

    def call(*args):
        return pl.pallas_call(
            body,
            in_specs=[smem()] + [vmem()] * n_in,
            out_specs=vmem() if single else [vmem()] * len(shapes),
            out_shape=shapes[0] if single else shapes,
            scratch_shapes=list(scratch),
            compiler_params=pltpu.CompilerParams(vmem_limit_bytes=limit),
        )(*args)

    return call


DEPTH = 12
QUAD = 4
NEAR, FAR = tuple(range(5)), tuple(range(5, COLS))


def densify_kernel(columns, ids_ref, table_ref, tiles_ref, out_ref, *scratch):
    acc_ref, buf_ref, sem_ref = scratch
    slots = 4 * len(columns)
    counts_at, width = tiles_ref.shape[1] * tiles_ref.shape[2], tiles_ref.shape[2]

    def place(slot):
        cls = slot // (2 * len(columns))
        k = columns[0] + lax.rem(slot // 2, len(columns))
        source, valid = slot_source(ids_ref, cls, k, lax.rem(slot, 2))
        offset = lax.bitwise_and(ids_ref[0] - source + 64, 63) - 32 * ids_ref[1]
        offset = jnp.where(valid, offset, 0)
        return offset, jnp.where(valid, table_ref[counts_at + offset], 0)

    def fetch(slot, act):
        offset, live = place(slot)
        at = lax.rem(slot, DEPTH)
        for i in range(0, width, QUAD):

            @pl.when(live > i)
            def _():
                act(
                    pltpu.make_async_copy(
                        tiles_ref.at[0, offset, pl.ds(i, QUAD)],
                        buf_ref.at[at, pl.ds(i, QUAD)],
                        sem_ref.at[at, i // QUAD],
                    )
                )

    def start(copy):
        copy.start()

    def wait(copy):
        copy.wait()

    for u in range(DEPTH):
        fetch(u, start)

    def body(slot, carry):
        at = lax.rem(slot, DEPTH)
        offset, live = place(slot)
        acc_ref[...] = jnp.zeros_like(acc_ref)
        fetch(slot, wait)

        def add(j, inner):
            code = table_ref[offset * width + j]
            acc_ref[code] += buf_ref[at, j].astype(jnp.float32)
            return inner

        lax.fori_loop(0, live, add, 0)

        @pl.when(slot + DEPTH < slots)
        def _():
            fetch(slot + DEPTH, start)

        for t in range(2):
            for s in range(2):
                out_ref[slot, t * 128 : (t + 1) * 128, s * 128 : (s + 1) * 128] = acc_ref[
                    t * 2 + s
                ].astype(jnp.bfloat16)
        return carry

    lax.fori_loop(0, slots, body, 0)


def densify(columns, ids, table, tile_values):
    return pl.pallas_call(
        functools.partial(densify_kernel, columns),
        in_specs=[smem()] * 2 + [pl.BlockSpec(memory_space=pltpu.HBM)],
        out_specs=vmem(),
        scratch_shapes=[
            pltpu.VMEM((4, 128, 128), jnp.float32),
            pltpu.VMEM((DEPTH,) + tile_values.shape[2:], jnp.bfloat16),
            pltpu.SemaphoreType.DMA((DEPTH, tile_values.shape[2] // QUAD)),
        ],
        out_shape=jax.ShapeDtypeStruct((4 * len(columns), 256, 256), jnp.bfloat16),
        compiler_params=pltpu.CompilerParams(vmem_limit_bytes=48 * MIB),
    )(ids, table, tile_values)


def join_kernel(ids_ref, *refs):
    for i, ref in enumerate(refs[:4]):
        for out in refs[4:] if i < 3 else refs[4:5]:
            out[i * GROUP : (i + 1) * GROUP, :] = ref[...]


def forward_kernel(columns, classes, first, ids_ref, *refs):
    split = 2 * len(classes)
    groups, (mats_ref, hub_ref), refs = refs[:split], refs[split : split + 2], refs[split + 2 :]
    before_ref, (out_ref, hot_ref, wts_ref, pick_ref) = (None, refs) if first else (refs[0], refs[1:])
    lane = lax.broadcasted_iota(jnp.int32, (2 * HEAD, 128), 1)
    column = lax.broadcasted_iota(jnp.int32, (2 * HEAD, 256), 1)
    total = None if first else before_ref[...]
    for n, cls in enumerate(classes):
        for i, k in enumerate(columns):
            if first:
                ref, base = groups[n * 2 + min(k, 1)], max(k - 1, 0) * GROUP
            else:
                ref, base = groups[n * 2 + i // 3], i % 3 * GROUP
            head = ref[base + 512 : base + GROUP, :].astype(jnp.float32)
            mine = jnp.sum(jnp.where(lane == ids_ref[0], head, 0.0), axis=1, keepdims=True)
            hot = (mine.astype(jnp.int32) == column).astype(jnp.float32).astype(jnp.bfloat16)
            for lr in range(2):
                slot = (n * len(columns) + i) * 2 + lr
                source, valid = slot_source(ids_ref, cls, k, lr)
                at = slice(slot * HEAD, (slot + 1) * HEAD)
                one = hot[lr * HEAD : (lr + 1) * HEAD, :]
                block = ref[base + lr * 256 : base + (lr + 1) * 256, :]
                both = dot(jnp.concatenate([mats_ref[(cls * len(columns) + i) * 2 + lr], one], axis=0), block)
                total = both[:256] if total is None else total + both[:256]
                hot_ref[at, :] = one
                pick_ref[at, :] = both[256:].astype(jnp.bfloat16)
                weights = hub_ref[source]
                wts_ref[at, :] = jnp.where(valid, weights, jnp.zeros_like(weights))
    out_ref[...] = (total + dot_tn(wts_ref[...], pick_ref[...])).astype(out_ref.dtype)


def forward(columns, classes, dtype, *args):
    rows = 2 * len(classes) * len(columns) * HEAD
    first = len(args) == 2 * len(classes) + 3
    return kernel_call(
        functools.partial(forward_kernel, columns, classes, first),
        len(args) - 1,
        [((256, 128), dtype), ((rows, 256), jnp.bfloat16), ((rows, 256), jnp.bfloat16)],
        scratch=[pltpu.VMEM((rows, 128), jnp.bfloat16)],
        limit=20 * MIB,
    )(*args)


def middle_kernel(
    ids_ref, mine_ref, theirs_ref, feat_ref, sw_ref, nw_ref, ct_ref, bias_ref, other_ref, *outs
):
    out_ref, grad_ref, self_ref, keep_ref, give_ref, sums_ref = outs
    feats = feat_ref[...]
    agg = mine_ref[...].astype(jnp.float32) + theirs_ref[...].astype(jnp.float32)
    agg = agg.astype(jnp.bfloat16)

    def half(sw, nw, ct, bias):
        pre = dot(feats, sw) + dot(agg, nw) + bias
        gate = jax.nn.sigmoid(pre)
        act = ct.astype(jnp.float32) * gate * (1.0 + pre * (1.0 - gate))
        return pre * gate, act.astype(jnp.bfloat16)

    sw, nw = sw_ref[...], nw_ref[...]
    sw2, nw2 = other_ref[0:128, :], other_ref[128:256, :]
    extra = other_ref[512:528, :].astype(jnp.float32)
    bias2 = extra[0:1] + extra[1:2] + extra[2:3]
    value, act = half(sw, nw, ct_ref[...], bias_ref[...])
    _, act2 = half(sw2, nw2, other_ref[256:512, :], bias2)
    out_ref[...] = value.astype(jnp.bfloat16)
    grad_ref[...] = (dot_nt(nw, act) + dot_nt(nw2, act2)).astype(jnp.bfloat16)
    self_ref[...] = dot_nt(sw, act) + dot_nt(sw2, act2)
    sums_ref[0:128, :] = dot_tn(act, feats)
    sums_ref[128:256, :] = dot_tn(act, agg)
    bias_sum = jnp.sum(act.astype(jnp.float32), axis=0, keepdims=True)
    low = lax.bitwise_and(ids_ref[0], 3)
    for lr in range(2):
        for cls, ref in enumerate((keep_ref, give_ref)):
            quarter = lax.bitwise_xor(low, 2 * lr + cls)
            ref[lr, 0:64, :] = sums_ref[pl.ds(pl.multiple_of(quarter * 64, 64), 64), :]
            ref[lr, 64:PART, :] = jnp.broadcast_to(bias_sum, (PART - 64, 128))


def middle(*args):
    return kernel_call(
        middle_kernel,
        8,
        [
            ((256, 128), jnp.bfloat16),
            ((128, 256), jnp.bfloat16),
            ((128, 256), jnp.float32),
            ((2, PART, 128), jnp.float32),
            ((2, PART, 128), jnp.float32),
        ],
        scratch=[pltpu.VMEM((256, 128), jnp.float32)],
    )(*args)


def backward_kernel(cls, columns, add, ids_ref, grad_ref, mats_ref, hot_ref, wts_ref, *refs):
    out_ref = refs[-1]
    grad = grad_ref[...]
    count = 2 * len(columns) * HEAD
    first = 0 if hot_ref.shape[0] == count else cls * count
    backs = dot_nt(wts_ref[first : first + count, :], grad).astype(jnp.bfloat16)
    for i in range(len(columns)):
        for lr in range(2):
            slot = (cls * len(columns) + i) * 2 + lr
            row = (2 * i + lr) * HEAD
            lanes = slice(lr * 256, (lr + 1) * 256)
            back = dot_tn(backs[row : row + HEAD], hot_ref[first + row : first + row + HEAD, :])
            part = dot(grad, mats_ref[slot]) + back
            if add:
                part += refs[0][i, :, lanes].astype(jnp.float32)
            out_ref[i, :, lanes] = part.astype(out_ref.dtype)


def backward(cls, columns, dtype, *args):
    body = functools.partial(backward_kernel, cls, columns, len(args) > 5)
    return kernel_call(body, len(args) - 1, ((len(columns), 128, 512), dtype), limit=20 * MIB)(
        *args
    )


def near_kernel(ids_ref, keep_ref, far_ref, *outs):
    for i, out in enumerate(outs):
        out[...] = (keep_ref[i + 1] + far_ref[i].astype(jnp.float32)).astype(jnp.bfloat16)


def mine_kernel(ids_ref, keep_ref, *refs):
    got, (same_ref, cross_ref) = refs[:4], refs[4:]
    total = keep_ref[0]
    for ref in got:
        total += ref[...].astype(jnp.float32)
    same_ref[...] = total[:, :256].astype(jnp.bfloat16)
    cross_ref[...] = total[:, 256:].astype(jnp.bfloat16)


def finish_kernel(scale, ids_ref, *refs):
    f32 = jnp.float32
    same_ref, rep_ref, down_ref, up_ref, add_ref = refs[:5]
    parts, (grad_ref, self_ref, neighbor_ref, bias_ref, sums_ref, bias_sums_ref) = refs[5:9], refs[9:]
    total = (same_ref[...].astype(f32) + rep_ref[...].astype(f32)) + (
        down_ref[...].astype(f32) + up_ref[...].astype(f32)
    )
    grad_ref[...] = (total + add_ref[...]).T.astype(jnp.bfloat16)
    low = lax.bitwise_and(ids_ref[0], 3)
    for lr in range(2):
        for cls in range(2):
            part = parts[2 * cls + lr]
            quarter = lax.bitwise_xor(low, 2 * lr + cls)
            sums_ref[pl.ds(pl.multiple_of(quarter * 64, 64), 64), :] = part[0:64, :]
            bias_sums_ref[quarter] = part[64:PART, :]
    self_ref[...] = sums_ref[0:128, :].T * scale
    neighbor_ref[...] = sums_ref[128:256, :].T * scale
    bias_ref[...] = bias_sums_ref[0][0:1] * scale


def layer(
    features,
    tile_values,
    tile_target,
    tile_source,
    tile_count,
    hub_list,
    hub_count,
    hub_weight,
    self_weight,
    neighbor_weight,
    bias,
    cotangent,
):
    f32, bf16 = jnp.float32, jnp.bfloat16
    blocks = lax.axis_size("blk")
    ids = jnp.stack([lax.axis_index("blk"), lax.axis_index("rep")]).astype(jnp.int32)

    live = jnp.arange(HEAD, dtype=jnp.int32)[None, :] < hub_count[0][:, None]
    lists = jnp.where(live, hub_list[0], -1).astype(bf16).T
    lists = jnp.pad(lists, ((0, 0), (0, 128 - blocks)), constant_values=-1)
    theirs = permute(features, SWAP_Y)
    their_lists = permute(lists, SWAP_Y)

    bias_hi = as_bf16(bias)
    bias_mid = as_bf16(bias - bias_hi)
    bias_lo = bias - bias_hi - bias_mid
    bias_rows = jnp.stack([bias_hi, bias_mid, bias_lo]).astype(bf16)
    bias_rows = jnp.pad(bias_rows, ((0, 13), (0, 0)))
    packed = jnp.concatenate([self_weight, neighbor_weight, cotangent, bias_rows], axis=0)

    col0 = jnp.concatenate([features, theirs, lists, their_lists], axis=0)
    code = (tile_target[0] * 2 + tile_source[0]).reshape(-1)
    table = jnp.concatenate([code, tile_count[0]])
    col0, table, ids, packed = lax.optimization_barrier((col0, table, ids, packed))
    other = permute(packed, SWAP_R)
    cols = [permute(col0, FROM_COL[k]) for k in range(1, 5)]
    oth0 = permute(col0, SWAP_C)
    turn = permute(col0, inverse(FROM_COL[4]))
    cols, sent = kernel_call(
        join_kernel, 4, [((4 * GROUP, 128), bf16), ((3 * GROUP, 128), bf16)]
    )(ids, *cols)
    far = permute(sent, FROM_COL[4])
    last = permute(turn, inverse(FROM_COL[4]))
    oth1 = permute(cols, SWAP_C)
    mats_near = densify(NEAR, ids, table, tile_values)
    mats_far = densify(FAR, ids, table, tile_values)
    oth2 = permute(far, SWAP_C)
    oth3 = permute(last, SWAP_C)

    partial, hot_near, wts_near = forward(
        NEAR, (0, 1), f32, ids, col0, cols, oth0, oth1, mats_near, hub_weight
    )
    partial, *hub0 = forward(FAR, (0,), f32, ids, far, last, mats_far, hub_weight, partial)
    partial, *hub1 = forward(FAR, (1,), bf16, ids, oth2, oth3, mats_far, hub_weight, partial)
    theirs = permute(partial, SWAP_R)
    output, grad, self_grad, parts, give_parts = middle(
        ids,
        partial,
        theirs,
        features,
        self_weight,
        neighbor_weight,
        cotangent,
        bias[None, :],
        other,
    )

    with_near = (grad, mats_near, hot_near, wts_near)
    got_far = permute(backward(1, FAR, bf16, ids, grad, mats_far, *hub1), SWAP_C)
    got_near = permute(backward(1, NEAR, bf16, ids, *with_near), SWAP_C)
    got_parts = permute(give_parts, SWAP_C)
    sent = backward(0, FAR, bf16, ids, grad, mats_far, *hub0, got_far)
    far_sums = permute(sent, inverse(FROM_COL[4]))
    keep = backward(0, NEAR, f32, ids, *with_near, got_near)

    def added(*terms):
        while len(terms) > 1:
            terms = [a + b for a, b in zip(terms[::2], terms[1::2])]
        return terms[0]

    def over_columns(value, routes):
        return added(value, *(permute(value, p) for p in routes))

    parts = added(parts, got_parts)
    quarter = added(parts[0], permute(parts[1], SWAP_L))
    quarter = over_columns(quarter, SAME_X)
    far_sums, _ = lax.optimization_barrier((far_sums, quarter))

    piece = ((128, 512), bf16)
    near = kernel_call(near_kernel, 2, [piece] * 4)(ids, keep, far_sums)
    got = [permute(near[k - 1], inverse(FROM_COL[k])) for k in range(1, 5)]
    quarter = over_columns(quarter, SAME_Z)
    line = permute(quarter, SWAP_L)
    core0, core1 = permute(quarter, SWAP_C), permute(line, SWAP_C)
    piece = ((128, 256), bf16)
    same, cross = kernel_call(mine_kernel, 5, [piece] * 2)(ids, keep, *got)
    over = permute(same, SWAP_R)
    down = permute(cross, FROM_DOWN)
    up = permute(cross, FROM_UP)
    grad_input, grad_self, grad_neighbor, grad_bias = kernel_call(
        functools.partial(finish_kernel, 1.0 / math.sqrt(256 * blocks)),
        9,
        [((256, 128), bf16), ((128, 128), f32), ((128, 128), f32), ((1, 128), f32)],
        scratch=[pltpu.VMEM((256, 128), f32), pltpu.VMEM((4, PART - 64, 128), f32)],
    )(ids, same, over, down, up, self_grad, quarter, line, core0, core1)
    return output, grad_input, grad_self, grad_neighbor, grad_bias[0]


def solution(mesh):
    in_specs = (
        P("blk", None),
        P("blk", "rep", None, None, None),
        P("blk", "rep", None),
        P("blk", "rep", None),
        P("blk", "rep"),
        P("blk", None, None),
        P("blk", None),
        P(None, None, "blk"),
        P(None, "rep"),
        P(None, "rep"),
        P("rep"),
        P("blk", "rep"),
    )
    out_specs = (P("blk", "rep"), P("blk", None), P(None, "rep"), P(None, "rep"), P("rep"))
    return jax.shard_map(layer, mesh=mesh, in_specs=in_specs, out_specs=out_specs, check_vma=False)
```
